128 devices in a mesh: band: 4 (over x_hi, core), dom: 32 (over y, x_lo, z).
Axes of the slice: x: 4 (x_hi: 2, x_lo: 2; x = x_hi * 2 + x_lo), y: 4, z: 4, core: 2. Of those that a mesh axis runs over, the one named last changes fastest.
Arguments:
- orbitals: float32 [16, 128, 128, 128], P('band', 'dom'), may hold values from -24 to 24
- potential: float32 [128, 128, 128], P('dom'), may hold values from -1.25 to 1.25
- rotation: float32 [16, 16], replicated, may hold values from -1.5 to 1.5
Outputs:
- rotated: float32 [16, 128, 128, 128], P('band', 'dom')
- correlation: float32 [16, 16], P('band')
The draws below stay inside these ranges and needn't reach their ends.
All inputs are finite; a program needn't handle non-finite values.
Results may differ from the reference program's by a relative error of at most 0.00022.
Values sent between devices are 32-bit elements; how exact they have to be, the bound alone decides.
No kernel may reach another device: no remote copies, remote signals or barrier semaphores. Data moves between devices by JAX's collectives and lax.ppermute only.
A program may use at most 128 MiB of HBM per device.

```python
import math
import jax
import jax.numpy as jnp
from jax import lax

GX = 128
GY = 128
DEGREE = 8
NORB = 16
NZ = 128


def draw_orbitals(key, part):
    first_key, second_key = jax.random.split(key, 2)
    scales = jnp.exp(jax.random.uniform(first_key, (NORB, 1, 1, 1), jnp.float32, math.log(0.4), math.log(4.0)))
    values = jnp.clip(jax.random.normal(second_key, (NORB, NZ, GY, GX), jnp.float32), -6.0, 6.0)
    return values * scales


def draw_potential(key, part):
    heights = (jnp.arange(NZ).astype(jnp.float32) + 0.5) / NZ
    slope = (2.0 * heights - 1.0).reshape(NZ, 1, 1)
    rough = jax.random.uniform(key, (NZ, GY, GX), jnp.float32, -1.0, 1.0)
    return 0.75 * slope + 0.5 * rough


def noise(own_key, extent, spread, limit, dtype=jnp.bfloat16):
    values = spread * jax.random.normal(own_key, extent, jnp.float32)
    return jnp.clip(values, min=-limit, max=limit).astype(dtype)


def setup_inputs(seed: int = 0) -> dict:
    seeds = jax.random.split(jax.random.key(seed), 4)
    orbitals = draw_orbitals(jax.random.fold_in(seeds[3], 71), 0)
    potential = draw_potential(jax.random.fold_in(seeds[3], 71), 0)
    rotation = noise(seeds[2], (NORB, NORB), NORB ** -0.5, 1.5, jnp.float32)
    return dict(orbitals=orbitals, potential=potential, rotation=rotation)


CENTER = 4.5
HALF_WIDTH = 5.0


def hamiltonian(field, potential):
    near_sum = jnp.roll(field, 1, 0) + jnp.roll(field, -1, 0)
    near_sum = near_sum + jnp.roll(field, 1, 1) + jnp.roll(field, -1, 1)
    near_sum = near_sum + jnp.roll(field, 1, 2) + jnp.roll(field, -1, 2)
    far_sum = jnp.roll(field, 2, 0) + jnp.roll(field, -2, 0)
    far_sum = far_sum + jnp.roll(field, 2, 1) + jnp.roll(field, -2, 1)
    far_sum = far_sum + jnp.roll(field, 2, 2) + jnp.roll(field, -2, 2)
    laplace = -7.5 * field + (4.0 / 3.0) * near_sum - (1.0 / 12.0) * far_sum
    return -0.5 * laplace + potential * field


def filtered_one(start, potential):
    previous = jnp.zeros_like(start)
    current = start
    for number in range(DEGREE):
        factor = 1.0 / HALF_WIDTH if number == 0 else 2.0 / HALF_WIDTH
        result = factor * (hamiltonian(current, potential) - CENTER * current)
        if number > 0:
            result = result - previous
        previous = current
        current = result
    return current


def reference(orbitals, potential, rotation):
    filtered = lax.map(lambda single: filtered_one(single, potential), orbitals)
    flat = filtered.reshape(NORB, -1)
    rotated = jnp.dot(rotation.T, flat, precision=lax.Precision.HIGHEST, preferred_element_type=jnp.float32)
    cells = NZ * GY * GX
    gram = jnp.dot(flat, flat.T, precision=lax.Precision.HIGHEST, preferred_element_type=jnp.float32) / cells
    left = jnp.dot(rotation.T, gram, precision=lax.Precision.HIGHEST, preferred_element_type=jnp.float32)
    correlation = jnp.dot(left, rotation, precision=lax.Precision.HIGHEST, preferred_element_type=jnp.float32)
    return rotated.reshape(filtered.shape), correlation
```

```python
import jax
import jax.numpy as jnp
import numpy as np
from jax import lax
from jax.experimental import pallas as pl
from jax.experimental.pallas import tpu as pltpu
from jax.sharding import Mesh, PartitionSpec as P

DEGREE = 8
CENTER = 4.5
HALF_WIDTH = 5.0
AXES = ("x_hi", "core", "y", "x_lo", "z")
SIZES = (2, 2, 4, 2, 4)
N = 128
PAD = 8
ROWS = N + 2 * PAD
OWN = 16
SPAN = 3 * OWN


def moved(array, where):
    pairs = []
    for i in range(int(np.prod(SIZES))):
        c = dict(zip(AXES, (int(k) for k in np.unravel_index(i, SIZES))))
        d = where(c)
        j = int(np.ravel_multi_index([d[a] % s for a, s in zip(AXES, SIZES)], SIZES))
        pairs.append((i, j))
    return lax.ppermute(array, AXES, pairs)


def to_orbital(shift):
    return lambda c: {**c, "core": c["x_lo"], "x_lo": c["core"], "z": c["z"] + shift}


def to_outer(c):
    return {**c, "core": 1 - c["core"], "y": c["y"] + (1 if c["core"] == 1 else -1)}


def to_sibling(c):
    return {**c, "core": 1 - c["core"]}


def to_home(a, e):
    return lambda c: {
        **c,
        "x_hi": c["x_hi"] ^ a,
        "core": c["x_lo"] ^ e,
        "x_lo": c["core"],
    }


FACTOR = 2.0 / HALF_WIDTH
DIAG = FACTOR * (0.5 * 7.5 - CENTER)
NEAR = FACTOR * (-0.5 * 4.0 / 3.0)
FAR = -1.0 / 16.0


def filter_kernel(place, *refs):
    blocks = refs[:12]
    out = refs[12]
    one, two, pot, sems, out_sem = refs[13:]
    core = place[0]
    z = place[1]
    rows = pl.ds(PAD, N)
    copies = []
    for part in range(3):
        offset = [OWN, 2 * OWN * (1 - core), 2 * OWN * core][part]
        for shift in range(4):
            ref = blocks[4 * part + shift]
            first = offset + 4 * lax.rem(z + 4 - shift, 4)
            for kind, target in ((0, one), (1, pot)):
                n = len(copies)
                copies.append(
                    pltpu.make_async_copy(
                        ref.at[pl.ds(4 * kind, 4)],
                        target.at[pl.ds(first, 4), rows, :],
                        sems.at[n],
                    )
                )
    for copy in copies:
        copy.start()
    for copy in copies:
        copy.wait()

    @pl.loop(0, SPAN)
    def _(p):
        one[p, 0:PAD, :] = one[p, N : N + PAD, :]
        one[p, N + PAD : ROWS, :] = one[p, PAD : 2 * PAD, :]
        pot[p, PAD : PAD + N, :] = FACTOR * pot[p, PAD : PAD + N, :] + DIAG

    for step in range(1, DEGREE + 1):
        src, dst = (one, two) if step % 2 == 1 else (two, one)

        @pl.loop(0, (SPAN - 4 * step) // 4)
        def _(group):
            p = 2 * step + 4 * group
            for t in range(N // 8):
                r = PAD + 8 * t
                column = [src[p + k - 2, r : r + 8, :] for k in range(8)]
                for k in range(4):
                    v = column[k + 2]
                    near = column[k + 1] + column[k + 3]
                    far = column[k] + column[k + 4]
                    near = near + (src[p + k, r - 1 : r + 7, :] + src[p + k, r + 1 : r + 9, :])
                    far = far + (src[p + k, r - 2 : r + 6, :] + src[p + k, r + 2 : r + 10, :])
                    near = near + (pltpu.roll(v, 1, 1) + pltpu.roll(v, N - 1, 1))
                    far = far + (pltpu.roll(v, 2, 1) + pltpu.roll(v, N - 2, 1))
                    res = pot[p + k, r : r + 8, :] * v + NEAR * (near + FAR * far)
                    if step == 1:
                        res = 0.5 * res
                    else:
                        res = res - dst[p + k, r : r + 8, :]
                    dst[p + k, r : r + 8, :] = res
                    if t == 0:
                        dst[p + k, N + PAD : ROWS, :] = res
                    if t == N // 8 - 1:
                        dst[p + k, 0:PAD, :] = res

    last = one if DEGREE % 2 == 0 else two
    copies = []
    for n in range(OWN):
        q = 4 * (n % 4) + n // 4
        copies.append(
            pltpu.make_async_copy(last.at[OWN + q, rows, :], out.at[n], out_sem.at[n])
        )
    for copy in copies:
        copy.start()
    for copy in copies:
        copy.wait()


def filtered(place, blocks):
    anywhere = pl.BlockSpec(memory_space=pl.ANY)
    return pl.pallas_call(
        filter_kernel,
        out_shape=jax.ShapeDtypeStruct((OWN, N, N), jnp.float32),
        grid_spec=pltpu.PrefetchScalarGridSpec(
            num_scalar_prefetch=1,
            grid=(1,),
            in_specs=[anywhere] * 12,
            out_specs=anywhere,
            scratch_shapes=[pltpu.VMEM((SPAN, ROWS, N), jnp.float32)] * 3
            + [pltpu.SemaphoreType.DMA((24,)), pltpu.SemaphoreType.DMA((OWN,))],
        ),
        compiler_params=pltpu.CompilerParams(vmem_limit_bytes=40 << 20),
        name="chebyshev",
    )(place, *blocks)


def rotate_kernel(place, rotation, x, o0, o1, o2, o3, gram, rot):
    band = place[0]
    outs = (o0, o1, o2, o3)
    for rel in range(4):
        b = band ^ rel

        @pl.loop(0, 4)
        def _(j, rel=rel, b=b):
            col = 4 * b + j
            coeffs = [rotation[i, col] for i in range(16)]

            @pl.loop(0, 4)
            def _(tt):
                for u in range(4):
                    r = pl.multiple_of(32 * tt + 8 * u, 8)
                    total = coeffs[0] * x[0, pl.ds(r, 8), :]
                    for i in range(1, 16):
                        total = total + coeffs[i] * x[i, pl.ds(r, 8), :]
                    outs[rel][j, pl.ds(r, 8), :] = total
                    rot[col, pl.ds(r, 8), :] = total

    @pl.loop(0, 16)
    def _(j):
        sums = [jnp.zeros((8, N), jnp.float32) for _ in range(16)]
        for t in range(N // 8):
            a = rot[j, 8 * t : 8 * t + 8, :]
            sums = [s + a * rot[k, 8 * t : 8 * t + 8, :] for k, s in enumerate(sums)]
        for k in range(16):
            gram[j, k : k + 1, :] = jnp.sum(sums[k], axis=0, keepdims=True)


def rotated_parts(place, rotation, planes):
    vmem = pl.BlockSpec(memory_space=pltpu.VMEM)
    smem = pl.BlockSpec(memory_space=pltpu.SMEM)
    part = jax.ShapeDtypeStruct((4, N, N), jnp.float32)
    return pl.pallas_call(
        rotate_kernel,
        out_shape=[part] * 4 + [jax.ShapeDtypeStruct((16, 16, N), jnp.float32)],
        in_specs=[smem, smem, vmem],
        out_specs=[vmem] * 5,
        scratch_shapes=[pltpu.VMEM((16, N, N), jnp.float32)],
        compiler_params=pltpu.CompilerParams(vmem_limit_bytes=32 << 20),
        name="rotate",
    )(place, rotation, planes)


def local(orbitals, potential, rotation):
    x_hi = lax.axis_index("x_hi")
    core = lax.axis_index("core")
    x_lo = lax.axis_index("x_lo")
    z = lax.axis_index("z")
    order = (0, 2, 1, 3)
    own = {}
    for shift in order:
        orbital = lax.dynamic_index_in_dim(orbitals, (z + shift) % 4, 0, keepdims=False)
        block = jnp.concatenate([orbital, potential], axis=0)
        own[shift] = moved(block, to_orbital(shift))
    outer = {s: moved(own[s], to_outer) for s in order}
    sibling = {s: moved(own[s], to_sibling) for s in order}
    place = jnp.stack([core, z]).astype(jnp.int32)
    blocks = [d[s] for d in (own, sibling, outer) for s in range(4)]
    mine = filtered(place, blocks)
    planes = lax.all_to_all(mine, ("x_hi", "x_lo", "z"), 0, 0, tiled=True)
    *parts, gram = rotated_parts(
        jnp.stack([2 * x_hi + x_lo]).astype(jnp.int32), rotation, planes
    )
    home = [moved(parts[2 * a + e], to_home(a, e)) for a in range(2) for e in range(2)]
    rows = jnp.sum(gram, axis=2).reshape(4, 64)
    rows = jnp.pad(rows, ((0, 0), (0, 64)))
    rows = jnp.broadcast_to(rows[:, None], (4, 32, 128)).reshape(128, 128)
    rows = lax.all_to_all(rows, AXES, 0, 0, tiled=True)
    correlation = (jnp.sum(rows, axis=0)[:64] / (N * N * N)).reshape(4, 16)
    band = 2 * x_hi + core
    pieces = []
    for p in range(4):
        rel = band ^ p
        piece = jnp.where(
            rel < 2,
            jnp.where(rel == 0, home[0], home[1]),
            jnp.where(rel == 2, home[2], home[3]),
        )
        pieces.append(piece)
    return jnp.stack(pieces, axis=1), correlation


def solution(mesh):
    fine = Mesh(mesh.devices.reshape(SIZES), AXES)
    band, dom = ("x_hi", "core"), ("y", "x_lo", "z")
    return jax.shard_map(
        local,
        mesh=fine,
        in_specs=(P(band, dom, None, None), P(dom, None, None), P()),
        out_specs=(P(band, dom, None, None), P(band, None)),
        check_vma=False,
    )
```

```python
import jax
import jax.numpy as jnp
import numpy as np
from jax import lax
from jax.experimental import pallas as pl
from jax.experimental.pallas import tpu as pltpu
from jax.sharding import Mesh, PartitionSpec as P

DEGREE = 8
CENTER = 4.5
HALF_WIDTH = 5.0
AXES = ("x_hi", "core", "y", "x_lo", "z")
SIZES = (2, 2, 4, 2, 4)
N = 128
PAD = 8
ROWS = N + 2 * PAD
OWN = 16


def moved(array, where):
    pairs = []
    for i in range(int(np.prod(SIZES))):
        c = dict(zip(AXES, (int(k) for k in np.unravel_index(i, SIZES))))
        d = where(c)
        j = int(np.ravel_multi_index([d[a] % s for a, s in zip(AXES, SIZES)], SIZES))
        pairs.append((i, j))
    return lax.ppermute(array, AXES, pairs)


def to_orbital(shift):
    return lambda c: {**c, "core": c["x_lo"], "x_lo": c["core"], "z": c["z"] + shift}


def to_outer(c):
    return {**c, "core": 1 - c["core"], "y": c["y"] + (1 if c["core"] == 1 else -1)}


def to_sibling(c):
    return {**c, "core": 1 - c["core"]}


def to_home(a, e):
    return lambda c: {
        **c,
        "x_hi": c["x_hi"] ^ a,
        "core": c["x_lo"] ^ e,
        "x_lo": c["core"],
    }


FACTOR = 2.0 / HALF_WIDTH
DIAG = FACTOR * (0.5 * 7.5 - CENTER)
NEAR = FACTOR * (-0.5 * 4.0 / 3.0)
UNIT = NEAR / 16.0


def stencil_matrix():
    m = np.zeros((N, N), np.float32)
    for i in range(N):
        for d, c in ((1, 16.0), (-1, 16.0), (2, -1.0), (-2, -1.0)):
            m[i, (i + d) % N] += c
    return jnp.asarray(np.concatenate([m, m], axis=0), jnp.bfloat16)


def place_blocks(ref, target, first, z, sems, copies):
    for shift in range(4):
        where = first + 4 * lax.rem(z + 4 - shift, 4)
        copies.append(
            pltpu.make_async_copy(
                ref.at[pl.ds(4 * shift, 4)],
                target.at[pl.ds(where, 4), pl.ds(PAD, N), :],
                sems.at[len(copies)],
            )
        )


def wrap_rows(ref, p):
    ref[p, 0:PAD, :] = ref[p, N : N + PAD, :]
    ref[p, N + PAD : ROWS, :] = ref[p, PAD : 2 * PAD, :]


def four_planes(src, dst, pot, along, matrix, p, first_step):
    for k in range(4):
        v = src[p + k, PAD : PAD + N, :]
        high = v.astype(jnp.bfloat16)
        low = (v - high.astype(jnp.float32)).astype(jnp.bfloat16)
        along[k] = jnp.dot(
            jnp.concatenate([high, low], axis=1),
            matrix[...],
            preferred_element_type=jnp.float32,
        )
    for t in range(N // 8):
        r = PAD + 8 * t
        column = [src[p + k - 2, r : r + 8, :] for k in range(8)]
        for k in range(4):
            near = column[k + 1] + column[k + 3]
            far = column[k] + column[k + 4]
            near = near + (src[p + k, r - 1 : r + 7, :] + src[p + k, r + 1 : r + 9, :])
            far = far + (src[p + k, r - 2 : r + 6, :] + src[p + k, r + 2 : r + 10, :])
            sums = (16.0 * near - far) + along[k, 8 * t : 8 * t + 8, :]
            res = pot[p + k, r : r + 8, :] * column[k + 2] + UNIT * sums
            if first_step:
                res = 0.5 * res
            else:
                res = res - dst[p + k, r : r + 8, :]
            dst[p + k, r : r + 8, :] = res
            if t == 0:
                dst[p + k, N + PAD : ROWS, :] = res
            if t == N // 8 - 1:
                dst[p + k, 0:PAD, :] = res


def inner_kernel(
    place, own, sibling, own_pot, sibling_pot, matrix, edges, one, two, pot, along, keep, sems, out_sems
):
    core, z = place[0], place[1]
    copies = []
    place_blocks(own, one, OWN * core, z, sems, copies)
    place_blocks(own_pot, pot, OWN * core, z, sems, copies)
    place_blocks(sibling, one, OWN * (1 - core), z, sems, copies)
    place_blocks(sibling_pot, pot, OWN * (1 - core), z, sems, copies)
    for copy in copies:
        copy.start()
    for copy in copies:
        copy.wait()

    @pl.loop(0, 2 * OWN)
    def _(p):
        wrap_rows(one, p)
        pot[p, PAD : PAD + N, :] = FACTOR * pot[p, PAD : PAD + N, :] + DIAG

    sent = []
    for step in range(DEGREE):
        src, dst = (one, two) if step % 2 == 1 else (two, one)
        if step > 0:

            @pl.loop(0, (2 * OWN - 4 * step) // 4)
            def _(group):
                four_planes(src, dst, pot, along, matrix, 2 * step + 4 * group, step == 1)

        base = 2 * step + core * (28 - 4 * step)

        @pl.loop(0, 4)
        def _(k):
            keep[4 * step + k] = dst[base + k]

        copy = pltpu.make_async_copy(
            keep.at[pl.ds(4 * step, 4)], edges.at[pl.ds(4 * step, 4)], out_sems.at[step]
        )
        copy.start()
        sent.append(copy)
    for copy in sent:
        copy.wait()


def outer_kernel(
    place, outer, outer_pot, own_pot, edges, matrix, out, one, two, pot, along, keep, sems, out_sems
):
    core, z = place[0], place[1]
    copies = []
    place_blocks(outer, one, 18 * core, z, sems, copies)
    place_blocks(outer_pot, pot, 18 * core, z, sems, copies)
    place_blocks(own_pot, pot, 16 - 14 * core, z, sems, copies)
    copies.append(pltpu.make_async_copy(edges, keep, sems.at[len(copies)]))
    for copy in copies:
        copy.start()
    for copy in copies:
        copy.wait()

    @pl.loop(0, OWN)
    def _(p):
        wrap_rows(one, p + 18 * core)

    @pl.loop(2, 2 * OWN)
    def _(p):
        pot[p, PAD : PAD + N, :] = FACTOR * pot[p, PAD : PAD + N, :] + DIAG

    for step in range(1, DEGREE + 1):
        src, dst = (one, two) if step % 2 == 1 else (two, one)
        before = step - 1
        base = 16 + 2 * before - core * (2 + 4 * before)

        @pl.loop(0, 4)
        def _(k):
            src[base + k] = keep[4 * before + k]

        first = 2 * step + core * (18 - 4 * step)

        @pl.loop(0, OWN // 4)
        def _(group):
            four_planes(src, dst, pot, along, matrix, first + 4 * group, step == 1)

    last = one if DEGREE % 2 == 0 else two
    copies = []
    for n in range(OWN):
        q = 4 * (n % 4) + n // 4
        copies.append(
            pltpu.make_async_copy(
                last.at[16 - 14 * core + q, pl.ds(PAD, N), :], out.at[n], out_sems.at[n]
            )
        )
    for copy in copies:
        copy.start()
    for copy in copies:
        copy.wait()


def filter_call(kernel, name, planes, n_in, shape, updates, args):
    anywhere = pl.BlockSpec(memory_space=pl.ANY)
    return pl.pallas_call(
        kernel,
        out_shape=jax.ShapeDtypeStruct(shape, jnp.float32),
        in_specs=[pl.BlockSpec(memory_space=pltpu.SMEM)]
        + [anywhere] * n_in
        + [pl.BlockSpec(memory_space=pltpu.VMEM)],
        out_specs=anywhere,
        scratch_shapes=[pltpu.VMEM((planes, ROWS, N), jnp.float32)] * 3
        + [
            pltpu.VMEM((4, N, N), jnp.float32),
            pltpu.VMEM((4 * DEGREE, ROWS, N), jnp.float32),
            pltpu.SemaphoreType.DMA((16,)),
            pltpu.SemaphoreType.DMA((16,)),
        ],
        compiler_params=pltpu.CompilerParams(vmem_limit_bytes=40 << 20),
        cost_estimate=pl.CostEstimate(flops=updates, bytes_accessed=0, transcendentals=0),
        name=name,
    )(*args, stencil_matrix())


def filtered(place, own, sibling, outer, own_pot, sibling_pot, outer_pot):
    edges = filter_call(
        inner_kernel, "inner", 2 * OWN, 4, (4 * DEGREE, ROWS, N), 112,
        (place, own, sibling, own_pot, sibling_pot),
    )
    return filter_call(
        outer_kernel, "outer", 2 * OWN + 2, 4, (OWN, N, N), 128,
        (place, outer, outer_pot, own_pot, edges),
    )


def rotate_kernel(place, rotation, x, o0, o1, o2, o3):
    outs = (o0, o1, o2, o3)
    for rel in range(4):
        b = place[0] ^ rel

        @pl.loop(0, 4)
        def _(j, rel=rel, b=b):
            coeffs = [rotation[i, 4 * b + j] for i in range(16)]

            @pl.loop(0, 2)
            def _(half):
                rows = [pl.ds(pl.multiple_of(64 * half + 8 * u, 8), 8) for u in range(8)]
                totals = [coeffs[0] * x[0, r, :] for r in rows]
                for i in range(1, 16):
                    totals = [a + coeffs[i] * x[i, r, :] for a, r in zip(totals, rows)]
                for a, r in zip(totals, rows):
                    outs[rel][j, r, :] = a


def rotated_parts(place, rotation, planes):
    vmem = pl.BlockSpec(memory_space=pltpu.VMEM)
    smem = pl.BlockSpec(memory_space=pltpu.SMEM)
    return pl.pallas_call(
        rotate_kernel,
        out_shape=[jax.ShapeDtypeStruct((4, N, N), jnp.float32)] * 4,
        in_specs=[smem, smem, vmem],
        out_specs=[vmem] * 4,
        compiler_params=pltpu.CompilerParams(vmem_limit_bytes=32 << 20),
        name="rotate",
    )(place, rotation, planes)


def gram_kernel(place, o0, o1, o2, o3, out, sums):
    parts = (o0, o1, o2, o3)
    sums[...] = jnp.zeros_like(sums)
    for rel in range(4):
        for j in range(4):
            row = 16 * (4 * (place[0] ^ rel) + j)
            for other in range(rel + 1):
                totals = [jnp.zeros((8, N), jnp.float32) for _ in range(4)]
                for t in range(N // 8):
                    a = parts[rel][j, 8 * t : 8 * t + 8, :]
                    totals = [
                        s + a * parts[other][k, 8 * t : 8 * t + 8, :]
                        for k, s in enumerate(totals)
                    ]
                for k in range(4):
                    total = jnp.sum(totals[k], axis=0, keepdims=True)
                    column = 4 * (place[0] ^ other) + k
                    sums[pl.ds(row + column, 1), :] = total
                    if other < rel:
                        back = 16 * column + 4 * (place[0] ^ rel) + j
                        sums[pl.ds(back, 1), :] = total
    out[...] = lax.dot_general(
        jnp.ones((N, N), jnp.float32),
        sums[...],
        (((1,), (1,)), ((), ())),
        precision=lax.Precision.HIGHEST,
        preferred_element_type=jnp.float32,
    )


def gram_rows(place, parts):
    vmem = pl.BlockSpec(memory_space=pltpu.VMEM)
    smem = pl.BlockSpec(memory_space=pltpu.SMEM)
    return pl.pallas_call(
        gram_kernel,
        out_shape=jax.ShapeDtypeStruct((N, 256), jnp.float32),
        in_specs=[smem] + [vmem] * 4,
        out_specs=vmem,
        scratch_shapes=[pltpu.VMEM((256, N), jnp.float32)],
        compiler_params=pltpu.CompilerParams(vmem_limit_bytes=32 << 20),
        cost_estimate=pl.CostEstimate(
            flops=N * N * 256 * 200, bytes_accessed=2 << 20, transcendentals=0
        ),
        name="gram",
    )(place, *parts)


def local(orbitals, potential, rotation):
    x_hi = lax.axis_index("x_hi")
    core = lax.axis_index("core")
    x_lo = lax.axis_index("x_lo")
    z = lax.axis_index("z")
    place = jnp.stack([core, z]).astype(jnp.int32)
    pots = [moved(potential, to_orbital(s)) for s in range(4)]
    orbs = [
        moved(
            lax.dynamic_index_in_dim(orbitals, (z + s) % 4, 0, keepdims=False), to_orbital(s)
        )
        for s in range(4)
    ]
    own_pot = jnp.concatenate(pots, axis=0)
    own = jnp.concatenate(orbs, axis=0)
    mine = filtered(
        place,
        own,
        moved(own, to_sibling),
        moved(own, to_outer),
        own_pot,
        moved(own_pot, to_sibling),
        moved(own_pot, to_outer),
    )
    planes = lax.all_to_all(mine, ("x_hi", "x_lo", "z"), 0, 0, tiled=True)
    base = jnp.stack([2 * x_hi + x_lo]).astype(jnp.int32)
    parts = rotated_parts(base, rotation, planes)
    home = [moved(parts[2 * a + e], to_home(a, e)) for a in range(2) for e in range(2)]
    parts, home[0] = lax.optimization_barrier((parts, home[0]))
    rows = lax.all_to_all(gram_rows(base, parts), AXES, 0, 0, tiled=True)
    total = jnp.sum(rows, axis=0).reshape(16, 16) / (N * N * N)
    correlation = lax.dynamic_slice_in_dim(total, 4 * (2 * x_hi + core), 4, 0)
    band = 2 * x_hi + core
    pieces = []
    for p in range(4):
        rel = band ^ p
        piece = jnp.where(
            rel < 2,
            jnp.where(rel == 0, home[0], home[1]),
            jnp.where(rel == 2, home[2], home[3]),
        )
        pieces.append(piece)
    return jnp.stack(pieces, axis=1), correlation


def solution(mesh):
    fine = Mesh(mesh.devices.reshape(SIZES), AXES)
    band, dom = ("x_hi", "core"), ("y", "x_lo", "z")
    return jax.shard_map(
        local,
        mesh=fine,
        in_specs=(P(band, dom, None, None), P(dom, None, None), P()),
        out_specs=(P(band, dom, None, None), P(band, None)),
        check_vma=False,
    )
```

```python
import functools

import jax
import jax.numpy as jnp
import numpy as np
from jax import lax
from jax.experimental import pallas as pl
from jax.experimental.pallas import tpu as pltpu
from jax.sharding import Mesh, PartitionSpec as P

DEGREE = 8
CENTER = 4.5
HALF_WIDTH = 5.0
AXES = ("x_hi", "core", "y", "x_lo", "z")
SIZES = (2, 2, 4, 2, 4)
N = 128
PAD = 8
ROWS = N + 2 * PAD
OWN = 16


def moved(array, where):
    pairs = []
    for i in range(int(np.prod(SIZES))):
        c = dict(zip(AXES, (int(k) for k in np.unravel_index(i, SIZES))))
        d = where(c)
        j = int(np.ravel_multi_index([d[a] % s for a, s in zip(AXES, SIZES)], SIZES))
        pairs.append((i, j))
    return lax.ppermute(array, AXES, pairs)


def to_orbital(shift):
    return lambda c: {**c, "core": c["x_lo"], "x_lo": c["core"], "z": c["z"] + shift}


def to_outer(c):
    return {**c, "core": 1 - c["core"], "y": c["y"] + (1 if c["core"] == 1 else -1)}


def to_sibling(c):
    return {**c, "core": 1 - c["core"]}


def to_home(a, e):
    return lambda c: {
        **c,
        "x_hi": c["x_hi"] ^ a,
        "core": c["x_lo"] ^ e,
        "x_lo": c["core"],
    }


FACTOR = 2.0 / HALF_WIDTH
DIAG = FACTOR * (0.5 * 7.5 - CENTER)
NEAR = FACTOR * (-0.5 * 4.0 / 3.0)
UNIT = NEAR / 16.0


def stencil_matrix():
    m = np.zeros((N, N), np.float32)
    for i in range(N):
        for d, c in ((1, 16.0), (-1, 16.0), (2, -1.0), (-2, -1.0)):
            m[i, (i + d) % N] += c
    return jnp.asarray(np.concatenate([m, m], axis=0), jnp.bfloat16)


def place_blocks(ref, target, first, z, sems, copies):
    for shift in range(4):
        where = first + 4 * lax.rem(z + 4 - shift, 4)
        copies.append(
            pltpu.make_async_copy(
                ref.at[pl.ds(4 * shift, 4)],
                target.at[pl.ds(where, 4), pl.ds(PAD, N), :],
                sems.at[len(copies)],
            )
        )


def wrap_rows(ref, p):
    ref[p, 0:PAD, :] = ref[p, N : N + PAD, :]
    ref[p, N + PAD : ROWS, :] = ref[p, PAD : 2 * PAD, :]


def four_planes(src, dst, pot, along, matrix, p, first_step):
    for k in range(4):
        v = src[p + k, PAD : PAD + N, :]
        high = v.astype(jnp.bfloat16)
        low = (v - high.astype(jnp.float32)).astype(jnp.bfloat16)
        along[k] = jnp.dot(
            jnp.concatenate([high, low], axis=1),
            matrix[...],
            preferred_element_type=jnp.float32,
        )
    for t in range(N // 8):
        r = PAD + 8 * t
        column = [src[p + k - 2, r : r + 8, :] for k in range(8)]
        for k in range(4):
            near = column[k + 1] + column[k + 3]
            far = column[k] + column[k + 4]
            near = near + (src[p + k, r - 1 : r + 7, :] + src[p + k, r + 1 : r + 9, :])
            far = far + (src[p + k, r - 2 : r + 6, :] + src[p + k, r + 2 : r + 10, :])
            sums = (16.0 * near - far) + along[k, 8 * t : 8 * t + 8, :]
            res = pot[p + k, r : r + 8, :] * column[k + 2] + UNIT * sums
            if first_step:
                res = 0.5 * res
            else:
                res = res - dst[p + k, r : r + 8, :]
            dst[p + k, r : r + 8, :] = res
            if t == 0:
                dst[p + k, N + PAD : ROWS, :] = res
            if t == N // 8 - 1:
                dst[p + k, 0:PAD, :] = res


def inner_kernel(
    place, own, sibling, own_pot, sibling_pot, matrix, edges, one, two, pot, along, sems
):
    core, z = place[0], place[1]
    copies = []
    place_blocks(own, one, OWN * core, z, sems, copies)
    place_blocks(own_pot, pot, OWN * core, z, sems, copies)
    place_blocks(sibling, one, OWN * (1 - core), z, sems, copies)
    place_blocks(sibling_pot, pot, OWN * (1 - core), z, sems, copies)
    for copy in copies:
        copy.start()
    for copy in copies:
        copy.wait()

    @pl.loop(0, 2 * OWN)
    def _(p):
        wrap_rows(one, p)

    for step in range(DEGREE):
        src, dst = (one, two) if step % 2 == 1 else (two, one)
        if step > 0:

            @pl.loop(0, (2 * OWN - 4 * step) // 4)
            def _(group):
                four_planes(src, dst, pot, along, matrix, 2 * step + 4 * group, step == 1)

        base = 2 * step + core * (28 - 4 * step)

        @pl.loop(0, 4)
        def _(k):
            edges[4 * step + k] = dst[base + k]


def outer_kernel(
    place, outer, outer_pot, own_pot, edges, matrix, out, one, two, pot, along, sems
):
    core, z = place[0], place[1]
    copies = []
    place_blocks(outer, one, 18 * core, z, sems, copies)
    place_blocks(outer_pot, pot, 18 * core, z, sems, copies)
    place_blocks(own_pot, pot, 16 - 14 * core, z, sems, copies)
    for copy in copies:
        copy.start()
    for copy in copies:
        copy.wait()

    @pl.loop(0, OWN)
    def _(p):
        wrap_rows(one, p + 18 * core)

    for step in range(1, DEGREE + 1):
        src, dst = (one, two) if step % 2 == 1 else (two, one)
        before = step - 1
        base = 16 + 2 * before - core * (2 + 4 * before)

        @pl.loop(0, 4)
        def _(k):
            src[base + k] = edges[4 * before + k]

        first = 2 * step + core * (18 - 4 * step)

        @pl.loop(0, OWN // 4)
        def _(group):
            four_planes(src, dst, pot, along, matrix, first + 4 * group, step == 1)

    last = one if DEGREE % 2 == 0 else two
    copies = []
    for n in range(OWN):
        q = 4 * (n % 4) + n // 4
        copies.append(
            pltpu.make_async_copy(
                last.at[16 - 14 * core + q, pl.ds(PAD, N), :], out.at[n], sems.at[n]
            )
        )
    for copy in copies:
        copy.start()
    for copy in copies:
        copy.wait()


def filter_call(kernel, name, planes, places, shape, place_out, args):
    return pl.pallas_call(
        kernel,
        out_shape=jax.ShapeDtypeStruct(shape, jnp.float32),
        in_specs=[pl.BlockSpec(memory_space=pltpu.SMEM)]
        + [pl.BlockSpec(memory_space=m) for m in places]
        + [pl.BlockSpec(memory_space=pltpu.VMEM)],
        out_specs=pl.BlockSpec(memory_space=place_out),
        scratch_shapes=[pltpu.VMEM((planes, ROWS, N), jnp.float32)] * 3
        + [pltpu.VMEM((4, N, N), jnp.float32), pltpu.SemaphoreType.DMA((16,))],
        compiler_params=pltpu.CompilerParams(vmem_limit_bytes=40 << 20),
        cost_estimate=pl.CostEstimate(flops=1000, bytes_accessed=0, transcendentals=0),
        name=name,
    )(*args, stencil_matrix())


def filtered(place, own, sibling, outer, own_pot, sibling_pot, outer_pot):
    edges = filter_call(
        inner_kernel, "inner", 2 * OWN, [pl.ANY] * 4, (4 * DEGREE, ROWS, N), pltpu.VMEM,
        (place, own, sibling, own_pot, sibling_pot),
    )
    return filter_call(
        outer_kernel, "outer", 2 * OWN + 2, [pl.ANY] * 3 + [pltpu.VMEM], (OWN, N, N), pl.ANY,
        (place, outer, outer_pot, own_pot, edges),
    )


def rotate_kernel(first, place, rotation, x, *outs):
    for n, out in enumerate(outs):
        b = place[0] ^ (first + n)

        @pl.loop(0, 4)
        def _(j, out=out, b=b):
            coeffs = [rotation[i, 4 * b + j] for i in range(16)]

            @pl.loop(0, 2)
            def _(half):
                rows = [pl.ds(pl.multiple_of(64 * half + 8 * u, 8), 8) for u in range(8)]
                totals = [coeffs[0] * x[0, r, :] for r in rows]
                for i in range(1, 16):
                    totals = [a + coeffs[i] * x[i, r, :] for a, r in zip(totals, rows)]
                for a, r in zip(totals, rows):
                    out[j, r, :] = a


def rotated_parts(first, place, rotation, planes):
    vmem = pl.BlockSpec(memory_space=pltpu.VMEM)
    smem = pl.BlockSpec(memory_space=pltpu.SMEM)
    return pl.pallas_call(
        functools.partial(rotate_kernel, first),
        out_shape=[jax.ShapeDtypeStruct((4, N, N), jnp.float32)] * 2,
        in_specs=[smem, smem, vmem],
        out_specs=[vmem] * 2,
        compiler_params=pltpu.CompilerParams(vmem_limit_bytes=32 << 20),
        name="rotate",
    )(place, rotation, planes)


def gram_kernel(place, o0, o1, o2, o3, out, sums):
    parts = (o0, o1, o2, o3)
    sums[...] = jnp.zeros_like(sums)
    for rel in range(4):
        for j in range(4):
            row = 16 * (4 * (place[0] ^ rel) + j)
            for other in range(rel + 1):
                totals = [jnp.zeros((8, N), jnp.float32) for _ in range(4)]
                for t in range(N // 8):
                    a = parts[rel][j, 8 * t : 8 * t + 8, :]
                    totals = [
                        s + a * parts[other][k, 8 * t : 8 * t + 8, :]
                        for k, s in enumerate(totals)
                    ]
                for k in range(4):
                    total = jnp.sum(totals[k], axis=0, keepdims=True)
                    column = 4 * (place[0] ^ other) + k
                    sums[pl.ds(row + column, 1), :] = total
                    if other < rel:
                        back = 16 * column + 4 * (place[0] ^ rel) + j
                        sums[pl.ds(back, 1), :] = total
    out[...] = lax.dot_general(
        jnp.ones((8, N), jnp.float32),
        sums[...],
        (((1,), (1,)), ((), ())),
        precision=lax.Precision.HIGHEST,
        preferred_element_type=jnp.float32,
    )


def gram_rows(place, parts):
    vmem = pl.BlockSpec(memory_space=pltpu.VMEM)
    smem = pl.BlockSpec(memory_space=pltpu.SMEM)
    return pl.pallas_call(
        gram_kernel,
        out_shape=jax.ShapeDtypeStruct((8, 256), jnp.float32),
        in_specs=[smem] + [vmem] * 4,
        out_specs=vmem,
        scratch_shapes=[pltpu.VMEM((256, N), jnp.float32)],
        compiler_params=pltpu.CompilerParams(vmem_limit_bytes=32 << 20),
        name="gram",
    )(place, *parts)


def local(orbitals, potential, rotation):
    x_hi = lax.axis_index("x_hi")
    core = lax.axis_index("core")
    x_lo = lax.axis_index("x_lo")
    z = lax.axis_index("z")
    place = jnp.stack([core, z]).astype(jnp.int32)
    orbs = [
        moved(
            lax.dynamic_index_in_dim(orbitals, (z + s) % 4, 0, keepdims=False), to_orbital(s)
        )
        for s in range(4)
    ]
    diagonal = FACTOR * potential + DIAG
    pots = [moved(diagonal, to_orbital(s)) for s in range(4)]
    own = jnp.concatenate(orbs, axis=0)
    own_pot = jnp.concatenate(pots, axis=0)
    outer = moved(own, to_outer)
    sibling = moved(own, to_sibling)
    outer_pot = moved(own_pot, to_outer)
    sibling_pot = moved(own_pot, to_sibling)
    sibling, outer = lax.optimization_barrier((sibling, outer))
    mine = filtered(place, own, sibling, outer, own_pot, sibling_pot, outer_pot)
    planes = lax.all_to_all(mine, ("x_hi", "x_lo", "z"), 0, 0, tiled=True)
    base = jnp.stack([2 * x_hi + x_lo]).astype(jnp.int32)
    far = rotated_parts(2, base, rotation, planes)
    near = rotated_parts(0, base, rotation, planes)
    home = [None] * 4
    home[2], home[3] = moved(far[0], to_home(1, 0)), moved(far[1], to_home(1, 1))
    home[0], home[1] = moved(near[0], to_home(0, 0)), moved(near[1], to_home(0, 1))
    total = gram_rows(base, [*near, *far])
    for axis, bit in (("z", 1), ("z", 2), ("y", 1), ("y", 2), ("core", 1), ("x_lo", 1), ("x_hi", 1)):
        total = total + moved(total, lambda c: {**c, axis: c[axis] ^ bit})
    total = total[0].reshape(16, 16) / (N * N * N)
    correlation = lax.dynamic_slice_in_dim(total, 4 * (2 * x_hi + core), 4, 0)
    band = 2 * x_hi + core
    pieces = []
    for p in range(4):
        rel = band ^ p
        piece = jnp.where(
            rel < 2,
            jnp.where(rel == 0, home[0], home[1]),
            jnp.where(rel == 2, home[2], home[3]),
        )
        pieces.append(piece)
    return jnp.stack(pieces, axis=1), correlation


def solution(mesh):
    fine = Mesh(mesh.devices.reshape(SIZES), AXES)
    band, dom = ("x_hi", "core"), ("y", "x_lo", "z")
    return jax.shard_map(
        local,
        mesh=fine,
        in_specs=(P(band, dom, None, None), P(dom, None, None), P()),
        out_specs=(P(band, dom, None, None), P(band, None)),
        check_vma=False,
    )
```

```python
import functools

import jax
import jax.numpy as jnp
import numpy as np
from jax import lax
from jax.experimental import pallas as pl
from jax.experimental.pallas import tpu as pltpu
from jax.sharding import Mesh, PartitionSpec as P

DEGREE = 8
CENTER = 4.5
HALF_WIDTH = 5.0
AXES = ("x_hi", "core", "y", "x_lo", "z")
SIZES = (2, 2, 4, 2, 4)
N = 128
PAD = 8
ROWS = N + 2 * PAD
OWN = 16


def moved(array, where):
    pairs = []
    for i in range(int(np.prod(SIZES))):
        c = dict(zip(AXES, (int(k) for k in np.unravel_index(i, SIZES))))
        d = where(c)
        j = int(np.ravel_multi_index([d[a] % s for a, s in zip(AXES, SIZES)], SIZES))
        pairs.append((i, j))
    return lax.ppermute(array, AXES, pairs)


def to_orbital(shift):
    return lambda c: {**c, "core": c["x_lo"], "x_lo": c["core"], "z": c["z"] + shift}


def to_outer(c):
    return {**c, "core": 1 - c["core"], "y": c["y"] + (1 if c["core"] == 1 else -1)}


def to_outer_natively(c):
    return {**c, "x_lo": 1 - c["x_lo"], "y": c["y"] + (1 if c["x_lo"] == 1 else -1)}


def to_sibling(c):
    return {**c, "core": 1 - c["core"]}


def to_home(a, e):
    return lambda c: {
        **c,
        "x_hi": c["x_hi"] ^ a,
        "core": c["x_lo"] ^ e,
        "x_lo": c["core"],
    }


FACTOR = 2.0 / HALF_WIDTH
DIAG = FACTOR * (0.5 * 7.5 - CENTER)
NEAR = FACTOR * (-0.5 * 4.0 / 3.0)
UNIT = NEAR / 16.0


def stencil_matrix():
    m = np.zeros((N, N), np.float32)
    for i in range(N):
        for d, c in ((1, 16.0), (-1, 16.0), (2, -1.0), (-2, -1.0)):
            m[i, (i + d) % N] += c
    return jnp.asarray(np.concatenate([m, m], axis=0), jnp.bfloat16)


def place_blocks(refs, target, first, z, sems, copies):
    if not isinstance(refs, (list, tuple)):
        refs = [refs.at[pl.ds(4 * shift, 4)] for shift in range(4)]
    for shift in range(4):
        where = first + 4 * lax.rem(z + 4 - shift, 4)
        copies.append(
            pltpu.make_async_copy(
                refs[shift],
                target.at[pl.ds(where, 4), pl.ds(PAD, N), :],
                sems.at[len(copies)],
            )
        )


def wrap_rows(ref, p):
    ref[p, 0:PAD, :] = ref[p, N : N + PAD, :]
    ref[p, N + PAD : ROWS, :] = ref[p, PAD : 2 * PAD, :]


def four_planes(src, dst, pot, along, matrix, p, first_step):
    for k in range(4):
        v = src[p + k, PAD : PAD + N, :]
        high = v.astype(jnp.bfloat16)
        low = (v - high.astype(jnp.float32)).astype(jnp.bfloat16)
        along[k] = jnp.dot(
            jnp.concatenate([high, low], axis=1),
            matrix[...],
            preferred_element_type=jnp.float32,
        )
    for t in range(N // 8):
        r = PAD + 8 * t
        column = [src[p + k - 2, r : r + 8, :] for k in range(8)]
        for k in range(4):
            near = column[k + 1] + column[k + 3]
            far = column[k] + column[k + 4]
            near = near + (src[p + k, r - 1 : r + 7, :] + src[p + k, r + 1 : r + 9, :])
            far = far + (src[p + k, r - 2 : r + 6, :] + src[p + k, r + 2 : r + 10, :])
            sums = (16.0 * near - far) + along[k, 8 * t : 8 * t + 8, :]
            res = pot[p + k, r : r + 8, :] * column[k + 2] + UNIT * sums
            if first_step:
                res = 0.5 * res
            else:
                res = res - dst[p + k, r : r + 8, :]
            dst[p + k, r : r + 8, :] = res
            if t == 0:
                dst[p + k, N + PAD : ROWS, :] = res
            if t == N // 8 - 1:
                dst[p + k, 0:PAD, :] = res


def inner_kernel(
    place, own, sibling, own_pot, sibling_pot, matrix, edges, one, two, pot, along, sems
):
    core, z = place[0], place[1]
    copies = []
    place_blocks(own, one, OWN * core, z, sems, copies)
    place_blocks(own_pot, pot, OWN * core, z, sems, copies)
    place_blocks(sibling, one, OWN * (1 - core), z, sems, copies)
    place_blocks(sibling_pot, pot, OWN * (1 - core), z, sems, copies)
    for copy in copies:
        copy.start()
    for copy in copies:
        copy.wait()

    @pl.loop(0, 2 * OWN)
    def _(p):
        wrap_rows(one, p)

    for step in range(DEGREE):
        src, dst = (one, two) if step % 2 == 1 else (two, one)
        if step > 0:

            @pl.loop(0, (2 * OWN - 4 * step) // 4)
            def _(group):
                four_planes(src, dst, pot, along, matrix, 2 * step + 4 * group, step == 1)

        base = 2 * step + core * (28 - 4 * step)

        @pl.loop(0, 4)
        def _(k):
            edges[4 * step + k] = dst[base + k]


def outer_kernel(
    place, outer, q0, q1, q2, q3, own_pot, edges, matrix, out, one, two, pot, along, sems
):
    core, z = place[0], place[1]
    copies = []
    place_blocks(outer, one, 18 * core, z, sems, copies)
    place_blocks((q0, q1, q2, q3), pot, 18 * core, z, sems, copies)
    place_blocks(own_pot, pot, 16 - 14 * core, z, sems, copies)
    for copy in copies:
        copy.start()
    for copy in copies:
        copy.wait()

    @pl.loop(0, OWN)
    def _(p):
        wrap_rows(one, p + 18 * core)

    for step in range(1, DEGREE + 1):
        src, dst = (one, two) if step % 2 == 1 else (two, one)
        before = step - 1
        base = 16 + 2 * before - core * (2 + 4 * before)

        @pl.loop(0, 4)
        def _(k):
            src[base + k] = edges[4 * before + k]

        first = 2 * step + core * (18 - 4 * step)

        @pl.loop(0, OWN // 4)
        def _(group):
            four_planes(src, dst, pot, along, matrix, first + 4 * group, step == 1)

    last = one if DEGREE % 2 == 0 else two
    copies = []
    for n in range(OWN):
        q = 4 * (n % 4) + n // 4
        copies.append(
            pltpu.make_async_copy(
                last.at[16 - 14 * core + q, pl.ds(PAD, N), :], out.at[n], sems.at[n]
            )
        )
    for copy in copies:
        copy.start()
    for copy in copies:
        copy.wait()


def filter_call(kernel, name, planes, places, shape, place_out, args):
    return pl.pallas_call(
        kernel,
        out_shape=jax.ShapeDtypeStruct(shape, jnp.float32),
        in_specs=[pl.BlockSpec(memory_space=pltpu.SMEM)]
        + [pl.BlockSpec(memory_space=m) for m in places]
        + [pl.BlockSpec(memory_space=pltpu.VMEM)],
        out_specs=pl.BlockSpec(memory_space=place_out),
        scratch_shapes=[pltpu.VMEM((planes, ROWS, N), jnp.float32)] * 3
        + [pltpu.VMEM((4, N, N), jnp.float32), pltpu.SemaphoreType.DMA((16,))],
        compiler_params=pltpu.CompilerParams(vmem_limit_bytes=40 << 20),
        cost_estimate=pl.CostEstimate(flops=1000, bytes_accessed=0, transcendentals=0),
        name=name,
    )(*args, stencil_matrix())


def filtered(place, own, sibling, outer, own_pot, sibling_pot, outer_pots):
    edges = filter_call(
        inner_kernel, "inner", 2 * OWN, [pl.ANY] * 4, (4 * DEGREE, ROWS, N), pltpu.VMEM,
        (place, own, sibling, own_pot, sibling_pot),
    )
    return filter_call(
        outer_kernel, "outer", 2 * OWN + 2, [pl.ANY] * 6 + [pltpu.VMEM], (OWN, N, N), pl.ANY,
        (place, outer, *outer_pots, own_pot, edges),
    )


def rotate_kernel(first, place, rotation, x, *outs):
    for n, out in enumerate(outs):
        b = place[0] ^ (first + n)

        @pl.loop(0, 4)
        def _(j, out=out, b=b):
            coeffs = [rotation[i, 4 * b + j] for i in range(16)]

            @pl.loop(0, 2)
            def _(half):
                rows = [pl.ds(pl.multiple_of(64 * half + 8 * u, 8), 8) for u in range(8)]
                totals = [coeffs[0] * x[0, r, :] for r in rows]
                for i in range(1, 16):
                    totals = [a + coeffs[i] * x[i, r, :] for a, r in zip(totals, rows)]
                for a, r in zip(totals, rows):
                    out[j, r, :] = a


def rotated_parts(first, place, rotation, planes):
    vmem = pl.BlockSpec(memory_space=pltpu.VMEM)
    smem = pl.BlockSpec(memory_space=pltpu.SMEM)
    return pl.pallas_call(
        functools.partial(rotate_kernel, first),
        out_shape=[jax.ShapeDtypeStruct((4, N, N), jnp.float32)] * 2,
        in_specs=[smem, smem, vmem],
        out_specs=[vmem] * 2,
        compiler_params=pltpu.CompilerParams(vmem_limit_bytes=32 << 20),
        name="rotate",
    )(place, rotation, planes)


def gram_kernel(x, square, out, sums):
    for i in range(16):
        for first in range(0, i + 1, 4):
            others = range(first, min(first + 4, i + 1))
            totals = [jnp.zeros((8, N), jnp.float32) for _ in others]
            for t in range(N // 8):
                a = x[i, 8 * t : 8 * t + 8, :]
                totals = [
                    s + a * x[k, 8 * t : 8 * t + 8, :] for s, k in zip(totals, others)
                ]
            for k, total in zip(others, totals):
                total = jnp.sum(total, axis=0, keepdims=True)
                sums[16 * i + k : 16 * i + k + 1, :] = total
                if k < i:
                    sums[16 * k + i : 16 * k + i + 1, :] = total
    gram = lax.dot_general(
        jnp.ones((8, N), jnp.float32),
        sums[...],
        (((1,), (1,)), ((), ())),
        precision=lax.Precision.HIGHEST,
        preferred_element_type=jnp.float32,
    )
    out[...] = jnp.dot(
        gram, square[...], precision=lax.Precision.HIGHEST, preferred_element_type=jnp.float32
    )


def gram_row(planes, square):
    vmem = pl.BlockSpec(memory_space=pltpu.VMEM)
    return pl.pallas_call(
        gram_kernel,
        out_shape=jax.ShapeDtypeStruct((8, 256), jnp.float32),
        in_specs=[vmem] * 2,
        out_specs=vmem,
        scratch_shapes=[pltpu.VMEM((256, N), jnp.float32)],
        compiler_params=pltpu.CompilerParams(vmem_limit_bytes=32 << 20),
        name="gram",
    )(planes, square)


def local(orbitals, potential, rotation):
    x_hi = lax.axis_index("x_hi")
    core = lax.axis_index("core")
    x_lo = lax.axis_index("x_lo")
    z = lax.axis_index("z")
    place = jnp.stack([core, z]).astype(jnp.int32)
    orbs = [
        moved(
            lax.dynamic_index_in_dim(orbitals, (z + s) % 4, 0, keepdims=False), to_orbital(s)
        )
        for s in range(4)
    ]
    diagonal = FACTOR * potential + DIAG
    beyond = moved(diagonal, to_outer_natively)
    own = jnp.concatenate(orbs, axis=0)
    own, diagonal, beyond = lax.optimization_barrier((own, diagonal, beyond))
    outer = moved(own, to_outer)
    sibling = moved(own, to_sibling)
    pots, outer_pots = [None] * 4, []
    for s in (1, 3, 2, 0):
        sent = diagonal
        if s == 0:
            sent, sibling = lax.optimization_barrier((diagonal, sibling))
        pots[s] = moved(sent, to_orbital(s))
    for s in range(4):
        sent, pots[s] = lax.optimization_barrier((beyond, pots[s]))
        outer_pots.append(moved(sent, to_orbital(s)))
    pots, outer = lax.optimization_barrier((pots, outer))
    own_pot = jnp.concatenate(pots, axis=0)
    sibling_pot = moved(own_pot, to_sibling)
    mine = filtered(place, own, sibling, outer, own_pot, sibling_pot, outer_pots)
    planes = lax.all_to_all(mine, ("x_hi", "x_lo", "z"), 0, 0, tiled=True)
    base = jnp.stack([2 * x_hi + x_lo]).astype(jnp.int32)
    square = (rotation[:, None, :, None] * rotation[None, :, None, :]).reshape(256, 256)
    total = gram_row(planes, square)
    far = rotated_parts(2, base, rotation, planes)
    near = rotated_parts(0, base, rotation, planes)
    home = [None] * 4
    home[2], home[3] = moved(far[0], to_home(1, 0)), moved(far[1], to_home(1, 1))
    home[0], home[1] = moved(near[0], to_home(0, 0)), moved(near[1], to_home(0, 1))
    stages = (("z", 1), ("z", 2), ("y", 1), ("y", 2), ("core", 1), ("x_lo", 1), ("x_hi", 1))
    for axis, bit in stages:
        total = total + moved(total, lambda c: {**c, axis: c[axis] ^ bit})
    total = total[0].reshape(16, 16) / (N * N * N)
    correlation = lax.dynamic_slice_in_dim(total, 4 * (2 * x_hi + core), 4, 0)
    band = 2 * x_hi + core
    pieces = []
    for p in range(4):
        rel = band ^ p
        piece = jnp.where(
            rel < 2,
            jnp.where(rel == 0, home[0], home[1]),
            jnp.where(rel == 2, home[2], home[3]),
        )
        pieces.append(piece)
    return jnp.stack(pieces, axis=1), correlation


def solution(mesh):
    fine = Mesh(mesh.devices.reshape(SIZES), AXES)
    band, dom = ("x_hi", "core"), ("y", "x_lo", "z")
    return jax.shard_map(
        local,
        mesh=fine,
        in_specs=(P(band, dom, None, None), P(dom, None, None), P()),
        out_specs=(P(band, dom, None, None), P(band, None)),
        check_vma=False,
    )
```

```python
import functools

import jax
import jax.numpy as jnp
import numpy as np
from jax import lax
from jax.experimental import pallas as pl
from jax.experimental.pallas import tpu as pltpu
from jax.sharding import Mesh, PartitionSpec as P

DEGREE = 8
CENTER = 4.5
HALF_WIDTH = 5.0
AXES = ("x_hi", "core", "y", "x_lo", "z")
SIZES = (2, 2, 4, 2, 4)
N = 128
PAD = 8
ROWS = N + 2 * PAD
OWN = 16


def moved(array, where):
    pairs = []
    for i in range(int(np.prod(SIZES))):
        c = dict(zip(AXES, (int(k) for k in np.unravel_index(i, SIZES))))
        d = where(c)
        j = int(np.ravel_multi_index([d[a] % s for a, s in zip(AXES, SIZES)], SIZES))
        pairs.append((i, j))
    return lax.ppermute(array, AXES, pairs)


def to_orbital(shift):
    return lambda c: {**c, "core": c["x_lo"], "x_lo": c["core"], "z": c["z"] + shift}


def to_outer(c):
    return {**c, "core": 1 - c["core"], "y": c["y"] + (1 if c["core"] == 1 else -1)}


def pot_to_orbital(shift):
    return lambda c: {**to_orbital(shift)(c), "x_hi": c["x_hi"] ^ c["core"] ^ c["x_lo"]}


def to_sibling(c):
    return {**c, "core": 1 - c["core"]}


def to_home(a, e):
    return lambda c: {
        **c,
        "x_hi": c["x_hi"] ^ a,
        "core": c["x_lo"] ^ e,
        "x_lo": c["core"],
    }


FACTOR = 2.0 / HALF_WIDTH
DIAG = FACTOR * (0.5 * 7.5 - CENTER)
NEAR = FACTOR * (-0.5 * 4.0 / 3.0)
UNIT = NEAR / 16.0


def stencil_matrix():
    m = np.zeros((N, N), np.float32)
    for i in range(N):
        for d, c in ((1, 16.0), (-1, 16.0), (2, -1.0), (-2, -1.0)):
            m[i, (i + d) % N] += c
    return jnp.asarray(np.concatenate([m, m], axis=0), jnp.bfloat16)


def place_blocks(ref, target, first, z, sems, copies):
    for shift in range(4):
        where = first + 4 * lax.rem(z + 4 - shift, 4)
        copies.append(
            pltpu.make_async_copy(
                ref.at[pl.ds(4 * shift, 4)],
                target.at[pl.ds(where, 4), pl.ds(PAD, N), :],
                sems.at[len(copies)],
            )
        )


def wrap_rows(ref, p):
    ref[p, 0:PAD, :] = ref[p, N : N + PAD, :]
    ref[p, N + PAD : ROWS, :] = ref[p, PAD : 2 * PAD, :]


def four_planes(src, dst, pot, along, matrix, p, first_step):
    for k in range(4):
        v = src[p + k, PAD : PAD + N, :]
        high = v.astype(jnp.bfloat16)
        low = (v - high.astype(jnp.float32)).astype(jnp.bfloat16)
        along[k] = jnp.dot(
            jnp.concatenate([high, low], axis=1),
            matrix[...],
            preferred_element_type=jnp.float32,
        )
    for t in range(N // 8):
        r = PAD + 8 * t
        column = [src[p + k - 2, r : r + 8, :] for k in range(8)]
        for k in range(4):
            near = column[k + 1] + column[k + 3]
            far = column[k] + column[k + 4]
            near = near + (src[p + k, r - 1 : r + 7, :] + src[p + k, r + 1 : r + 9, :])
            far = far + (src[p + k, r - 2 : r + 6, :] + src[p + k, r + 2 : r + 10, :])
            sums = (16.0 * near - far) + along[k, 8 * t : 8 * t + 8, :]
            res = pot[p + k, r : r + 8, :] * column[k + 2] + UNIT * sums
            if first_step:
                res = 0.5 * res
            else:
                res = res - dst[p + k, r : r + 8, :]
            dst[p + k, r : r + 8, :] = res
            if t == 0:
                dst[p + k, N + PAD : ROWS, :] = res
            if t == N // 8 - 1:
                dst[p + k, 0:PAD, :] = res


def inner_kernel(
    place, own, sibling, own_pot, sibling_pot, matrix, edges, one, two, pot, along, sems
):
    core, z = place[0], place[1]
    copies = []
    place_blocks(own, one, OWN * core, z, sems, copies)
    place_blocks(own_pot, pot, OWN * core, z, sems, copies)
    place_blocks(sibling, one, OWN * (1 - core), z, sems, copies)
    place_blocks(sibling_pot, pot, OWN * (1 - core), z, sems, copies)
    for copy in copies:
        copy.start()
    for copy in copies:
        copy.wait()

    @pl.loop(0, 2 * OWN)
    def _(p):
        wrap_rows(one, p)

    for step in range(DEGREE):
        src, dst = (one, two) if step % 2 == 1 else (two, one)
        if step > 0:

            @pl.loop(0, (2 * OWN - 4 * step) // 4)
            def _(group):
                four_planes(src, dst, pot, along, matrix, 2 * step + 4 * group, step == 1)

        base = 2 * step + core * (28 - 4 * step)

        @pl.loop(0, 4)
        def _(k):
            edges[4 * step + k] = dst[base + k]


def outer_kernel(
    place, outer, outer_pot, own_pot, edges, matrix, out, one, two, pot, along, sems
):
    core, z = place[0], place[1]
    copies = []
    place_blocks(outer, one, 18 * core, z, sems, copies)
    place_blocks(outer_pot, pot, 18 * core, z, sems, copies)
    place_blocks(own_pot, pot, 16 - 14 * core, z, sems, copies)
    for copy in copies:
        copy.start()
    for copy in copies:
        copy.wait()

    @pl.loop(0, OWN)
    def _(p):
        wrap_rows(one, p + 18 * core)

    for step in range(1, DEGREE + 1):
        src, dst = (one, two) if step % 2 == 1 else (two, one)
        before = step - 1
        base = 16 + 2 * before - core * (2 + 4 * before)

        @pl.loop(0, 4)
        def _(k):
            src[base + k] = edges[4 * before + k]

        first = 2 * step + core * (18 - 4 * step)

        @pl.loop(0, OWN // 4)
        def _(group):
            four_planes(src, dst, pot, along, matrix, first + 4 * group, step == 1)

    last = one if DEGREE % 2 == 0 else two
    copies = []
    for n in range(OWN):
        q = 4 * (n % 4) + n // 4
        copies.append(
            pltpu.make_async_copy(
                last.at[16 - 14 * core + q, pl.ds(PAD, N), :], out.at[n], sems.at[n]
            )
        )
    for copy in copies:
        copy.start()
    for copy in copies:
        copy.wait()


def filter_call(kernel, name, planes, places, shape, place_out, args):
    return pl.pallas_call(
        kernel,
        out_shape=jax.ShapeDtypeStruct(shape, jnp.float32),
        in_specs=[pl.BlockSpec(memory_space=pltpu.SMEM)]
        + [pl.BlockSpec(memory_space=m) for m in places]
        + [pl.BlockSpec(memory_space=pltpu.VMEM)],
        out_specs=pl.BlockSpec(memory_space=place_out),
        scratch_shapes=[pltpu.VMEM((planes, ROWS, N), jnp.float32)] * 3
        + [pltpu.VMEM((4, N, N), jnp.float32), pltpu.SemaphoreType.DMA((16,))],
        compiler_params=pltpu.CompilerParams(vmem_limit_bytes=40 << 20),
        cost_estimate=pl.CostEstimate(flops=1000, bytes_accessed=0, transcendentals=0),
        name=name,
    )(*args, stencil_matrix())


def filtered(place, own, sibling, outer, own_pot, sibling_pot, outer_pot):
    edges = filter_call(
        inner_kernel, "inner", 2 * OWN, [pl.ANY] * 4, (4 * DEGREE, ROWS, N), pltpu.VMEM,
        (place, own, sibling, own_pot, sibling_pot),
    )
    return filter_call(
        outer_kernel, "outer", 2 * OWN + 2, [pl.ANY] * 3 + [pltpu.VMEM], (OWN, N, N), pl.ANY,
        (place, outer, outer_pot, own_pot, edges),
    )


def rotate_kernel(first, place, rotation, x, *outs):
    for n, out in enumerate(outs):
        b = place[0] ^ (first + n)

        @pl.loop(0, 4)
        def _(j, out=out, b=b):
            coeffs = [rotation[i, 4 * b + j] for i in range(16)]

            @pl.loop(0, 2)
            def _(half):
                rows = [pl.ds(pl.multiple_of(64 * half + 8 * u, 8), 8) for u in range(8)]
                totals = [coeffs[0] * x[0, r, :] for r in rows]
                for i in range(1, 16):
                    totals = [a + coeffs[i] * x[i, r, :] for a, r in zip(totals, rows)]
                for a, r in zip(totals, rows):
                    out[j, r, :] = a


def rotated_parts(first, place, rotation, planes):
    vmem = pl.BlockSpec(memory_space=pltpu.VMEM)
    smem = pl.BlockSpec(memory_space=pltpu.SMEM)
    return pl.pallas_call(
        functools.partial(rotate_kernel, first),
        out_shape=[jax.ShapeDtypeStruct((4, N, N), jnp.float32)] * 2,
        in_specs=[smem, smem, vmem],
        out_specs=[vmem] * 2,
        compiler_params=pltpu.CompilerParams(vmem_limit_bytes=32 << 20),
        name="rotate",
    )(place, rotation, planes)


def gram_kernel(x, square, out, sums):
    for i in range(16):
        for first in range(0, i + 1, 4):
            others = range(first, min(first + 4, i + 1))
            totals = [jnp.zeros((8, N), jnp.float32) for _ in others]
            for t in range(N // 8):
                a = x[i, 8 * t : 8 * t + 8, :]
                totals = [
                    s + a * x[k, 8 * t : 8 * t + 8, :] for s, k in zip(totals, others)
                ]
            for k, total in zip(others, totals):
                total = jnp.sum(total, axis=0, keepdims=True)
                sums[16 * i + k : 16 * i + k + 1, :] = total
                if k < i:
                    sums[16 * k + i : 16 * k + i + 1, :] = total
    gram = lax.dot_general(
        jnp.ones((16, N), jnp.float32),
        sums[...],
        (((1,), (1,)), ((), ())),
        precision=lax.Precision.HIGHEST,
        preferred_element_type=jnp.float32,
    )
    out[...] = jnp.dot(
        gram, square[...], precision=lax.Precision.HIGHEST, preferred_element_type=jnp.float32
    )


def gram_row(planes, square):
    vmem = pl.BlockSpec(memory_space=pltpu.VMEM)
    return pl.pallas_call(
        gram_kernel,
        out_shape=jax.ShapeDtypeStruct((16, 256), jnp.float32),
        in_specs=[vmem] * 2,
        out_specs=vmem,
        scratch_shapes=[pltpu.VMEM((256, N), jnp.float32)],
        compiler_params=pltpu.CompilerParams(vmem_limit_bytes=32 << 20),
        name="gram",
    )(planes, square)


def local(orbitals, potential, rotation):
    x_hi = lax.axis_index("x_hi")
    core = lax.axis_index("core")
    x_lo = lax.axis_index("x_lo")
    z = lax.axis_index("z")
    place = jnp.stack([core, z]).astype(jnp.int32)
    orbs = [
        moved(
            lax.dynamic_index_in_dim(orbitals, (z + s) % 4, 0, keepdims=False), to_orbital(s)
        )
        for s in range(4)
    ]
    diagonal = FACTOR * potential + DIAG
    own = jnp.concatenate(orbs, axis=0)
    own, diagonal = lax.optimization_barrier((own, diagonal))
    outer = moved(own, to_outer)
    sibling = moved(own, to_sibling)
    pots = [None] * 4
    for s in (1, 3, 2, 0):
        sent = diagonal
        if s == 0:
            sent, sibling = lax.optimization_barrier((diagonal, sibling))
        pots[s] = moved(sent, pot_to_orbital(s))
    pots, outer = lax.optimization_barrier((pots, outer))
    own_pot = jnp.concatenate(pots, axis=0)
    outer_pot = moved(own_pot, to_outer)
    sibling_pot = moved(own_pot, to_sibling)
    mine = filtered(place, own, sibling, outer, own_pot, sibling_pot, outer_pot)
    planes = lax.all_to_all(mine, ("x_hi", "x_lo", "z"), 0, 0, tiled=True)
    base = jnp.stack([2 * x_hi + x_lo]).astype(jnp.int32)
    square = (rotation[:, None, :, None] * rotation[None, :, None, :]).reshape(256, 256)
    rows = lax.all_to_all(gram_row(planes, square), ("y", "z"), 0, 0, tiled=True)
    far = rotated_parts(2, base, rotation, planes)
    near = rotated_parts(0, base, rotation, planes)
    home = [None] * 4
    home[2], home[3] = moved(far[0], to_home(1, 0)), moved(far[1], to_home(1, 1))
    home[0], home[1] = moved(near[0], to_home(0, 0)), moved(near[1], to_home(0, 1))
    total = jnp.sum(rows, axis=0, keepdims=True)
    total, home[0] = lax.optimization_barrier((total, home[0]))
    for axis in ("core", "x_lo", "x_hi"):
        total = total + moved(total, lambda c: {**c, axis: 1 - c[axis]})
    total = total.reshape(16, 16) / (N * N * N)
    correlation = lax.dynamic_slice_in_dim(total, 4 * (2 * x_hi + core), 4, 0)
    band = 2 * x_hi + core
    pieces = []
    for p in range(4):
        rel = band ^ p
        piece = jnp.where(
            rel < 2,
            jnp.where(rel == 0, home[0], home[1]),
            jnp.where(rel == 2, home[2], home[3]),
        )
        pieces.append(piece)
    return jnp.stack(pieces, axis=1), correlation


def solution(mesh):
    fine = Mesh(mesh.devices.reshape(SIZES), AXES)
    band, dom = ("x_hi", "core"), ("y", "x_lo", "z")
    return jax.shard_map(
        local,
        mesh=fine,
        in_specs=(P(band, dom, None, None), P(dom, None, None), P()),
        out_specs=(P(band, dom, None, None), P(band, None)),
        check_vma=False,
    )
```

```python
import functools

import jax
import jax.numpy as jnp
import numpy as np
from jax import lax
from jax.experimental import pallas as pl
from jax.experimental.pallas import tpu as pltpu
from jax.sharding import Mesh, PartitionSpec as P

DEGREE = 8
CENTER = 4.5
HALF_WIDTH = 5.0
AXES = ("x_hi", "core", "y", "x_lo", "z")
SIZES = (2, 2, 4, 2, 4)
N = 128
PAD = 8
ROWS = N + 2 * PAD
OWN = 16


def moved(array, where):
    pairs = []
    for i in range(int(np.prod(SIZES))):
        c = dict(zip(AXES, (int(k) for k in np.unravel_index(i, SIZES))))
        d = where(c)
        j = int(np.ravel_multi_index([d[a] % s for a, s in zip(AXES, SIZES)], SIZES))
        pairs.append((i, j))
    return lax.ppermute(array, AXES, pairs)


def to_orbital(shift):
    return lambda c: {**c, "core": c["x_lo"], "x_lo": c["core"], "z": c["z"] + shift}


def to_outer(c):
    return {**c, "core": 1 - c["core"], "y": c["y"] + (1 if c["core"] == 1 else -1)}


def pot_to_orbital(shift):
    return lambda c: {**to_orbital(shift)(c), "x_hi": c["x_hi"] ^ c["core"] ^ c["x_lo"]}


def to_sibling(c):
    return {**c, "core": 1 - c["core"]}


def to_home(a, e):
    return lambda c: {
        **c,
        "x_hi": c["x_hi"] ^ a,
        "core": c["x_lo"] ^ e,
        "x_lo": c["core"],
    }


FACTOR = 2.0 / HALF_WIDTH
DIAG = FACTOR * (0.5 * 7.5 - CENTER)
NEAR = FACTOR * (-0.5 * 4.0 / 3.0)
UNIT = NEAR / 16.0


def stencil_matrix():
    m = np.zeros((N, N), np.float32)
    for i in range(N):
        for d, c in ((1, 16.0), (-1, 16.0), (2, -1.0), (-2, -1.0)):
            m[i, (i + d) % N] += c
    return jnp.asarray(np.concatenate([m, m], axis=0), jnp.bfloat16)


def place_blocks(ref, target, first, z, sems, copies):
    for shift in range(4):
        where = first + 4 * lax.rem(z + 4 - shift, 4)
        copies.append(
            pltpu.make_async_copy(
                ref.at[pl.ds(4 * shift, 4)],
                target.at[pl.ds(where, 4), pl.ds(PAD, N), :],
                sems.at[len(copies)],
            )
        )


def wrap_rows(ref, p):
    ref[p, 0:PAD, :] = ref[p, N : N + PAD, :]
    ref[p, N + PAD : ROWS, :] = ref[p, PAD : 2 * PAD, :]


def products(src, along, matrix, p):
    for k in range(4):
        v = src[p + k, PAD : PAD + N, :]
        high = v.astype(jnp.bfloat16)
        low = (v - high.astype(jnp.float32)).astype(jnp.bfloat16)
        along[k] = jnp.dot(
            jnp.concatenate([high, low], axis=1),
            matrix[...],
            preferred_element_type=jnp.float32,
        )


def four_planes(src, dst, pot, along, p, first_step):
    for t in range(N // 8):
        r = PAD + 8 * t
        column = [src[p + k - 2, r : r + 8, :] for k in range(8)]
        for k in range(4):
            near = column[k + 1] + column[k + 3]
            far = column[k] + column[k + 4]
            near = near + (src[p + k, r - 1 : r + 7, :] + src[p + k, r + 1 : r + 9, :])
            far = far + (src[p + k, r - 2 : r + 6, :] + src[p + k, r + 2 : r + 10, :])
            sums = (16.0 * near - far) + along[k, 8 * t : 8 * t + 8, :]
            res = pot[p + k, r : r + 8, :] * column[k + 2] + UNIT * sums
            if first_step:
                res = 0.5 * res
            else:
                res = res - dst[p + k, r : r + 8, :]
            dst[p + k, r : r + 8, :] = res
            if t == 0:
                dst[p + k, N + PAD : ROWS, :] = res
            if t == N // 8 - 1:
                dst[p + k, 0:PAD, :] = res


def advance(src, dst, pot, along, matrix, first, count, first_step):
    products(src, along[0], matrix, first)
    for group in range(count // 4):
        p = first + 4 * group
        if 4 * group + 4 < count:
            products(src, along[(group + 1) % 2], matrix, p + 4)
        four_planes(src, dst, pot, along[group % 2], p, first_step)


def inner_kernel(
    place, own, sibling, own_pot, sibling_pot, matrix, edges, one, two, pot, even, odd, sems
):
    core, z = place[0], place[1]
    copies = []
    place_blocks(own, one, OWN * core, z, sems, copies)
    place_blocks(own_pot, pot, OWN * core, z, sems, copies)
    place_blocks(sibling, one, OWN * (1 - core), z, sems, copies)
    place_blocks(sibling_pot, pot, OWN * (1 - core), z, sems, copies)
    for copy in copies:
        copy.start()
    for copy in copies:
        copy.wait()

    @pl.loop(0, 2 * OWN)
    def _(p):
        wrap_rows(one, p)

    for step in range(DEGREE):
        src, dst = (one, two) if step % 2 == 1 else (two, one)
        if step > 0:
            advance(
                src, dst, pot, (even, odd), matrix, 2 * step, 2 * OWN - 4 * step, step == 1
            )

        base = 2 * step + core * (28 - 4 * step)

        @pl.loop(0, 4)
        def _(k):
            edges[4 * step + k] = dst[base + k]


def outer_kernel(
    place, outer, outer_pot, own_pot, edges, matrix, out, one, two, pot, even, odd, sems
):
    core, z = place[0], place[1]
    copies = []
    place_blocks(outer, one, 18 * core, z, sems, copies)
    place_blocks(outer_pot, pot, 18 * core, z, sems, copies)
    place_blocks(own_pot, pot, 16 - 14 * core, z, sems, copies)
    for copy in copies:
        copy.start()
    for copy in copies:
        copy.wait()

    @pl.loop(0, OWN)
    def _(p):
        wrap_rows(one, p + 18 * core)

    for step in range(1, DEGREE + 1):
        src, dst = (one, two) if step % 2 == 1 else (two, one)
        before = step - 1
        base = 16 + 2 * before - core * (2 + 4 * before)

        @pl.loop(0, 4)
        def _(k):
            src[base + k] = edges[4 * before + k]

        first = 2 * step + core * (18 - 4 * step)
        advance(src, dst, pot, (even, odd), matrix, first, OWN, step == 1)

    last = one if DEGREE % 2 == 0 else two
    copies = []
    for n in range(OWN):
        q = 4 * (n % 4) + n // 4
        copies.append(
            pltpu.make_async_copy(
                last.at[16 - 14 * core + q, pl.ds(PAD, N), :], out.at[n], sems.at[n]
            )
        )
    for copy in copies:
        copy.start()
    for copy in copies:
        copy.wait()


def filter_call(kernel, name, planes, places, shape, place_out, args):
    return pl.pallas_call(
        kernel,
        out_shape=jax.ShapeDtypeStruct(shape, jnp.float32),
        in_specs=[pl.BlockSpec(memory_space=pltpu.SMEM)]
        + [pl.BlockSpec(memory_space=m) for m in places]
        + [pl.BlockSpec(memory_space=pltpu.VMEM)],
        out_specs=pl.BlockSpec(memory_space=place_out),
        scratch_shapes=[pltpu.VMEM((planes, ROWS, N), jnp.float32)] * 3
        + [pltpu.VMEM((4, N, N), jnp.float32)] * 2
        + [pltpu.SemaphoreType.DMA((16,))],
        compiler_params=pltpu.CompilerParams(vmem_limit_bytes=40 << 20),
        cost_estimate=pl.CostEstimate(flops=1000, bytes_accessed=0, transcendentals=0),
        name=name,
    )(*args, stencil_matrix())


def filtered(place, own, sibling, outer, own_pot, sibling_pot, outer_pot):
    edges = filter_call(
        inner_kernel, "inner", 2 * OWN, [pl.ANY] * 4, (4 * DEGREE, ROWS, N), pltpu.VMEM,
        (place, own, sibling, own_pot, sibling_pot),
    )
    return filter_call(
        outer_kernel, "outer", 2 * OWN + 2, [pl.ANY] * 3 + [pltpu.VMEM], (OWN, N, N), pl.ANY,
        (place, outer, outer_pot, own_pot, edges),
    )


def rotate_kernel(first, place, rotation, x, *outs):
    for n, out in enumerate(outs):
        b = place[0] ^ (first + n)

        @pl.loop(0, 4)
        def _(j, out=out, b=b):
            coeffs = [rotation[i, 4 * b + j] for i in range(16)]

            @pl.loop(0, 2)
            def _(half):
                rows = [pl.ds(pl.multiple_of(64 * half + 8 * u, 8), 8) for u in range(8)]
                totals = [coeffs[0] * x[0, r, :] for r in rows]
                for i in range(1, 16):
                    totals = [a + coeffs[i] * x[i, r, :] for a, r in zip(totals, rows)]
                for a, r in zip(totals, rows):
                    out[j, r, :] = a


def rotated_parts(first, place, rotation, planes):
    vmem = pl.BlockSpec(memory_space=pltpu.VMEM)
    smem = pl.BlockSpec(memory_space=pltpu.SMEM)
    return pl.pallas_call(
        functools.partial(rotate_kernel, first),
        out_shape=[jax.ShapeDtypeStruct((4, N, N), jnp.float32)] * 2,
        in_specs=[smem, smem, vmem],
        out_specs=[vmem] * 2,
        compiler_params=pltpu.CompilerParams(vmem_limit_bytes=32 << 20),
        name="rotate",
    )(place, rotation, planes)


def gram_kernel(place, o0, o1, o2, o3, out, sums):
    parts = (o0, o1, o2, o3)
    sums[...] = jnp.zeros_like(sums)
    for rel in range(4):
        for j in range(4):
            row = 16 * (4 * (place[0] ^ rel) + j)
            for other in range(rel + 1):
                totals = [jnp.zeros((8, N), jnp.float32) for _ in range(4)]
                for t in range(N // 8):
                    a = parts[rel][j, 8 * t : 8 * t + 8, :]
                    totals = [
                        s + a * parts[other][k, 8 * t : 8 * t + 8, :]
                        for k, s in enumerate(totals)
                    ]
                for k in range(4):
                    total = jnp.sum(totals[k], axis=0, keepdims=True)
                    column = 4 * (place[0] ^ other) + k
                    sums[pl.ds(row + column, 1), :] = total
                    if other < rel:
                        back = 16 * column + 4 * (place[0] ^ rel) + j
                        sums[pl.ds(back, 1), :] = total
    out[...] = lax.dot_general(
        jnp.ones((16, N), jnp.float32),
        sums[...],
        (((1,), (1,)), ((), ())),
        precision=lax.Precision.HIGHEST,
        preferred_element_type=jnp.float32,
    )


def gram_rows(place, parts):
    vmem = pl.BlockSpec(memory_space=pltpu.VMEM)
    smem = pl.BlockSpec(memory_space=pltpu.SMEM)
    return pl.pallas_call(
        gram_kernel,
        out_shape=jax.ShapeDtypeStruct((16, 256), jnp.float32),
        in_specs=[smem] + [vmem] * 4,
        out_specs=vmem,
        scratch_shapes=[pltpu.VMEM((256, N), jnp.float32)],
        compiler_params=pltpu.CompilerParams(vmem_limit_bytes=32 << 20),
        name="gram",
    )(place, *parts)


def local(orbitals, potential, rotation):
    x_hi = lax.axis_index("x_hi")
    core = lax.axis_index("core")
    x_lo = lax.axis_index("x_lo")
    z = lax.axis_index("z")
    place = jnp.stack([core, z]).astype(jnp.int32)
    orbs = [
        moved(
            lax.dynamic_index_in_dim(orbitals, (z + s) % 4, 0, keepdims=False), to_orbital(s)
        )
        for s in range(4)
    ]
    diagonal = FACTOR * potential + DIAG
    pots = [moved(diagonal, pot_to_orbital(s)) for s in range(4)]
    own = jnp.concatenate(orbs, axis=0)
    own_pot = jnp.concatenate(pots, axis=0)
    outer = moved(own, to_outer)
    sibling = moved(own, to_sibling)
    outer_pot = moved(own_pot, to_outer)
    sibling_pot = moved(own_pot, to_sibling)
    sibling, outer = lax.optimization_barrier((sibling, outer))
    mine = filtered(place, own, sibling, outer, own_pot, sibling_pot, outer_pot)
    planes = lax.all_to_all(mine, ("x_hi", "x_lo", "z"), 0, 0, tiled=True)
    base = jnp.stack([2 * x_hi + x_lo]).astype(jnp.int32)
    far = rotated_parts(2, base, rotation, planes)
    far, planes = lax.optimization_barrier((far, planes))
    near = rotated_parts(0, base, rotation, planes)
    home = [None] * 4
    home[2], home[3] = moved(far[0], to_home(1, 0)), moved(far[1], to_home(1, 1))
    home[0], home[1] = moved(near[0], to_home(0, 0)), moved(near[1], to_home(0, 1))
    rows = lax.all_to_all(gram_rows(base, [*near, *far]), ("y", "z"), 0, 0, tiled=True)
    total = jnp.sum(rows, axis=0, keepdims=True)
    total, home[0] = lax.optimization_barrier((total, home[0]))
    for axis in ("core", "x_lo", "x_hi"):
        total = total + moved(total, lambda c: {**c, axis: 1 - c[axis]})
    total = total.reshape(16, 16) / (N * N * N)
    correlation = lax.dynamic_slice_in_dim(total, 4 * (2 * x_hi + core), 4, 0)
    band = 2 * x_hi + core
    pieces = []
    for p in range(4):
        rel = band ^ p
        piece = jnp.where(
            rel < 2,
            jnp.where(rel == 0, home[0], home[1]),
            jnp.where(rel == 2, home[2], home[3]),
        )
        pieces.append(piece)
    return jnp.stack(pieces, axis=1), correlation


def solution(mesh):
    fine = Mesh(mesh.devices.reshape(SIZES), AXES)
    band, dom = ("x_hi", "core"), ("y", "x_lo", "z")
    return jax.shard_map(
        local,
        mesh=fine,
        in_specs=(P(band, dom, None, None), P(dom, None, None), P()),
        out_specs=(P(band, dom, None, None), P(band, None)),
        check_vma=False,
    )
```

```python
import jax
import jax.numpy as jnp
import numpy as np
from jax import lax
from jax.experimental import pallas as pl
from jax.experimental.pallas import tpu as pltpu
from jax.sharding import Mesh, PartitionSpec as P

DEGREE = 8
CENTER = 4.5
HALF_WIDTH = 5.0
AXES = ("x_hi", "core", "y", "x_lo", "z")
SIZES = (2, 2, 4, 2, 4)
N = 128
PAD = 8
ROWS = N + 2 * PAD
OWN = 16


def moved(array, where):
    pairs = []
    for i in range(int(np.prod(SIZES))):
        c = dict(zip(AXES, (int(k) for k in np.unravel_index(i, SIZES))))
        d = where(c)
        j = int(np.ravel_multi_index([d[a] % s for a, s in zip(AXES, SIZES)], SIZES))
        pairs.append((i, j))
    return lax.ppermute(array, AXES, pairs)


def to_orbital(shift):
    return lambda c: {**c, "core": c["x_lo"], "x_lo": c["core"], "z": c["z"] + shift}


def to_outer(c):
    return {**c, "core": 1 - c["core"], "y": c["y"] + (1 if c["core"] == 1 else -1)}


def pot_to_orbital(shift):
    return lambda c: {**to_orbital(shift)(c), "x_hi": c["x_hi"] ^ c["core"] ^ c["x_lo"]}


def to_sibling(c):
    return {**c, "core": 1 - c["core"]}


def to_home(a, e):
    return lambda c: {
        **c,
        "x_hi": c["x_hi"] ^ a,
        "core": c["x_lo"] ^ e,
        "x_lo": c["core"],
    }


FACTOR = 2.0 / HALF_WIDTH
DIAG = FACTOR * (0.5 * 7.5 - CENTER)
NEAR = FACTOR * (-0.5 * 4.0 / 3.0)
UNIT = NEAR / 16.0


def stencil_matrix():
    m = np.zeros((N, N), np.float32)
    for i in range(N):
        for d, c in ((1, 16.0), (-1, 16.0), (2, -1.0), (-2, -1.0)):
            m[i, (i + d) % N] += c
    return jnp.asarray(np.concatenate([m, m], axis=0), jnp.bfloat16)


def place_blocks(ref, target, first, z, sems, copies):
    for shift in range(4):
        where = first + 4 * lax.rem(z + 4 - shift, 4)
        copies.append(
            pltpu.make_async_copy(
                ref.at[pl.ds(4 * shift, 4)],
                target.at[pl.ds(where, 4), pl.ds(PAD, N), :],
                sems.at[len(copies)],
            )
        )


def wrap_rows(ref, p):
    ref[p, 0:PAD, :] = ref[p, N : N + PAD, :]
    ref[p, N + PAD : ROWS, :] = ref[p, PAD : 2 * PAD, :]


def products(src, along, matrix, p):
    for k in range(4):
        v = src[p + k, PAD : PAD + N, :]
        high = v.astype(jnp.bfloat16)
        low = (v - high.astype(jnp.float32)).astype(jnp.bfloat16)
        along[k] = jnp.dot(
            jnp.concatenate([high, low], axis=1),
            matrix[...],
            preferred_element_type=jnp.float32,
        )


def four_planes(src, dst, pot, along, p, first_step):
    for t in range(N // 8):
        r = PAD + 8 * t
        column = [src[p + k - 2, r : r + 8, :] for k in range(8)]
        for k in range(4):
            near = column[k + 1] + column[k + 3]
            far = column[k] + column[k + 4]
            near = near + (src[p + k, r - 1 : r + 7, :] + src[p + k, r + 1 : r + 9, :])
            far = far + (src[p + k, r - 2 : r + 6, :] + src[p + k, r + 2 : r + 10, :])
            sums = (16.0 * near - far) + along[k, 8 * t : 8 * t + 8, :]
            res = pot[p + k, r : r + 8, :] * column[k + 2] + UNIT * sums
            if first_step:
                res = 0.5 * res
            else:
                res = res - dst[p + k, r : r + 8, :]
            dst[p + k, r : r + 8, :] = res
            if t == 0:
                dst[p + k, N + PAD : ROWS, :] = res
            if t == N // 8 - 1:
                dst[p + k, 0:PAD, :] = res


def advance(src, dst, pot, along, matrix, first, count, first_step):
    products(src, along[0], matrix, first)
    for group in range(count // 4):
        p = first + 4 * group
        if 4 * group + 4 < count:
            products(src, along[(group + 1) % 2], matrix, p + 4)
        four_planes(src, dst, pot, along[group % 2], p, first_step)


def inner_kernel(
    place, own, sibling, own_pot, sibling_pot, matrix, edges, one, two, pot, even, odd, sems
):
    core, z = place[0], place[1]
    copies = []
    place_blocks(own, one, OWN * core, z, sems, copies)
    place_blocks(own_pot, pot, OWN * core, z, sems, copies)
    place_blocks(sibling, one, OWN * (1 - core), z, sems, copies)
    place_blocks(sibling_pot, pot, OWN * (1 - core), z, sems, copies)
    for copy in copies:
        copy.start()
    for copy in copies:
        copy.wait()

    @pl.loop(0, 2 * OWN)
    def _(p):
        wrap_rows(one, p)

    for step in range(DEGREE):
        src, dst = (one, two) if step % 2 == 1 else (two, one)
        if step > 0:
            advance(
                src, dst, pot, (even, odd), matrix, 2 * step, 2 * OWN - 4 * step, step == 1
            )

        base = 2 * step + core * (28 - 4 * step)

        @pl.loop(0, 4)
        def _(k):
            edges[4 * step + k] = dst[base + k]


def outer_kernel(
    place, outer, outer_pot, own_pot, edges, matrix, out, one, two, pot, even, odd, sems
):
    core, z = place[0], place[1]
    copies = []
    place_blocks(outer, one, 18 * core, z, sems, copies)
    place_blocks(outer_pot, pot, 18 * core, z, sems, copies)
    place_blocks(own_pot, pot, 16 - 14 * core, z, sems, copies)
    for copy in copies:
        copy.start()
    for copy in copies:
        copy.wait()

    @pl.loop(0, OWN)
    def _(p):
        wrap_rows(one, p + 18 * core)

    for step in range(1, DEGREE + 1):
        src, dst = (one, two) if step % 2 == 1 else (two, one)
        before = step - 1
        base = 16 + 2 * before - core * (2 + 4 * before)

        @pl.loop(0, 4)
        def _(k):
            src[base + k] = edges[4 * before + k]

        first = 2 * step + core * (18 - 4 * step)
        advance(src, dst, pot, (even, odd), matrix, first, OWN, step == 1)

    last = one if DEGREE % 2 == 0 else two
    copies = []
    for n in range(OWN):
        q = 4 * (n % 4) + n // 4
        copies.append(
            pltpu.make_async_copy(
                last.at[16 - 14 * core + q, pl.ds(PAD, N), :], out.at[n], sems.at[n]
            )
        )
    for copy in copies:
        copy.start()
    for copy in copies:
        copy.wait()


def filter_call(kernel, name, planes, places, shape, place_out, args):
    return pl.pallas_call(
        kernel,
        out_shape=jax.ShapeDtypeStruct(shape, jnp.float32),
        in_specs=[pl.BlockSpec(memory_space=pltpu.SMEM)]
        + [pl.BlockSpec(memory_space=m) for m in places]
        + [pl.BlockSpec(memory_space=pltpu.VMEM)],
        out_specs=pl.BlockSpec(memory_space=place_out),
        scratch_shapes=[pltpu.VMEM((planes, ROWS, N), jnp.float32)] * 3
        + [pltpu.VMEM((4, N, N), jnp.float32)] * 2
        + [pltpu.SemaphoreType.DMA((16,))],
        compiler_params=pltpu.CompilerParams(vmem_limit_bytes=20 << 20),
        cost_estimate=pl.CostEstimate(flops=1000, bytes_accessed=0, transcendentals=0),
        name=name,
    )(*args, stencil_matrix())


def filtered(place, own, sibling, outer, own_pot, sibling_pot, outer_pot):
    edges = filter_call(
        inner_kernel, "inner", 2 * OWN, [pl.ANY] * 4, (4 * DEGREE, ROWS, N), pltpu.VMEM,
        (place, own, sibling, own_pot, sibling_pot),
    )
    return filter_call(
        outer_kernel, "outer", 2 * OWN + 2, [pl.ANY] * 3 + [pltpu.VMEM], (OWN, N, N), pl.ANY,
        (place, outer, outer_pot, own_pot, edges),
    )


def rotate_kernel(place, rotation, x, *outs):
    for n, out in enumerate(outs):
        b = place[0] ^ n

        @pl.loop(0, 4)
        def _(j, out=out, b=b):
            coeffs = [rotation[i, 4 * b + j] for i in range(16)]
            for first in range(0, N, 64):
                rows = [slice(first + 8 * u, first + 8 * u + 8) for u in range(8)]
                totals = [coeffs[0] * x[0, r, :] for r in rows]
                for i in range(1, 16):
                    totals = [a + coeffs[i] * x[i, r, :] for a, r in zip(totals, rows)]
                for a, r in zip(totals, rows):
                    out[j, r, :] = a


def rotated_parts(place, rotation, planes):
    vmem = pl.BlockSpec(memory_space=pltpu.VMEM)
    smem = pl.BlockSpec(memory_space=pltpu.SMEM)
    return pl.pallas_call(
        rotate_kernel,
        out_shape=[jax.ShapeDtypeStruct((4, N, N), jnp.float32)] * 4,
        in_specs=[smem, smem, vmem],
        out_specs=[vmem] * 4,
        compiler_params=pltpu.CompilerParams(vmem_limit_bytes=16 << 20),
        name="rotate",
    )(place, rotation, planes)


def gram_kernel(place, o0, o1, o2, o3, out, sums):
    parts = (o0, o1, o2, o3)
    sums[...] = jnp.zeros_like(sums)
    for rel in range(4):
        for j in range(4):
            row = 16 * (4 * (place[0] ^ rel) + j)
            for other in range(rel + 1):
                totals = [jnp.zeros((8, N), jnp.float32) for _ in range(4)]
                for t in range(N // 8):
                    a = parts[rel][j, 8 * t : 8 * t + 8, :]
                    totals = [
                        s + a * parts[other][k, 8 * t : 8 * t + 8, :]
                        for k, s in enumerate(totals)
                    ]
                for k in range(4):
                    total = jnp.sum(totals[k], axis=0, keepdims=True)
                    column = 4 * (place[0] ^ other) + k
                    sums[pl.ds(row + column, 1), :] = total
                    if other < rel:
                        back = 16 * column + 4 * (place[0] ^ rel) + j
                        sums[pl.ds(back, 1), :] = total
    out[...] = lax.dot_general(
        jnp.ones((N, N), jnp.float32),
        sums[...],
        (((1,), (1,)), ((), ())),
        precision=lax.Precision.HIGHEST,
        preferred_element_type=jnp.float32,
    )


def gram_rows(place, parts):
    vmem = pl.BlockSpec(memory_space=pltpu.VMEM)
    smem = pl.BlockSpec(memory_space=pltpu.SMEM)
    return pl.pallas_call(
        gram_kernel,
        out_shape=jax.ShapeDtypeStruct((N, 256), jnp.float32),
        in_specs=[smem] + [vmem] * 4,
        out_specs=vmem,
        scratch_shapes=[pltpu.VMEM((256, N), jnp.float32)],
        compiler_params=pltpu.CompilerParams(vmem_limit_bytes=16 << 20),
        name="gram",
    )(place, *parts)


def local(orbitals, potential, rotation):
    x_hi = lax.axis_index("x_hi")
    core = lax.axis_index("core")
    x_lo = lax.axis_index("x_lo")
    z = lax.axis_index("z")
    place = jnp.stack([core, z]).astype(jnp.int32)
    orbs = [
        moved(
            lax.dynamic_index_in_dim(orbitals, (z + s) % 4, 0, keepdims=False), to_orbital(s)
        )
        for s in range(4)
    ]
    diagonal = FACTOR * potential + DIAG
    pots = [moved(diagonal, pot_to_orbital(s)) for s in range(4)]
    own = jnp.concatenate(orbs, axis=0)
    own_pot = jnp.concatenate(pots, axis=0)
    outer = moved(own, to_outer)
    sibling = moved(own, to_sibling)
    outer_pot = moved(own_pot, to_outer)
    sibling_pot = moved(own_pot, to_sibling)
    sibling, outer = lax.optimization_barrier((sibling, outer))
    mine = filtered(place, own, sibling, outer, own_pot, sibling_pot, outer_pot)
    planes = lax.all_to_all(mine, ("x_hi", "x_lo", "z"), 0, 0, tiled=True)
    base = jnp.stack([2 * x_hi + x_lo]).astype(jnp.int32)
    parts = rotated_parts(base, rotation, planes)
    home = [moved(parts[2 * a + e], to_home(a, e)) for a in range(2) for e in range(2)]
    parts, home[0] = lax.optimization_barrier((parts, home[0]))
    rows = lax.all_to_all(gram_rows(base, parts), AXES, 0, 0, tiled=True)
    total = jnp.sum(rows, axis=0)
    total = total.reshape(16, 16) / (N * N * N)
    correlation = lax.dynamic_slice_in_dim(total, 4 * (2 * x_hi + core), 4, 0)
    band = 2 * x_hi + core
    pieces = []
    for p in range(4):
        rel = band ^ p
        piece = jnp.where(
            rel < 2,
            jnp.where(rel == 0, home[0], home[1]),
            jnp.where(rel == 2, home[2], home[3]),
        )
        pieces.append(piece)
    return jnp.stack(pieces, axis=1), correlation


def solution(mesh):
    fine = Mesh(mesh.devices.reshape(SIZES), AXES)
    band, dom = ("x_hi", "core"), ("y", "x_lo", "z")
    return jax.shard_map(
        local,
        mesh=fine,
        in_specs=(P(band, dom, None, None), P(dom, None, None), P()),
        out_specs=(P(band, dom, None, None), P(band, None)),
        check_vma=False,
    )
```

```python
import jax
import jax.numpy as jnp
import numpy as np
from jax import lax
from jax.experimental import pallas as pl
from jax.experimental.pallas import tpu as pltpu
from jax.sharding import Mesh, PartitionSpec as P

DEGREE = 8
CENTER = 4.5
HALF_WIDTH = 5.0
AXES = ("x_hi", "core", "y", "x_lo", "z")
SIZES = (2, 2, 4, 2, 4)
N = 128
PAD = 8
ROWS = N + 2 * PAD
OWN = 16


def moved(array, where):
    pairs = []
    for i in range(int(np.prod(SIZES))):
        c = dict(zip(AXES, (int(k) for k in np.unravel_index(i, SIZES))))
        d = where(c)
        j = int(np.ravel_multi_index([d[a] % s for a, s in zip(AXES, SIZES)], SIZES))
        pairs.append((i, j))
    return lax.ppermute(array, AXES, pairs)


def to_orbital(shift):
    return lambda c: {**c, "core": c["x_lo"], "x_lo": c["core"], "z": c["z"] + shift}


def to_outer(c):
    return {**c, "core": 1 - c["core"], "y": c["y"] + (1 if c["core"] == 1 else -1)}


def pot_to_orbital(shift):
    return lambda c: {**to_orbital(shift)(c), "x_hi": c["x_hi"] ^ c["core"] ^ c["x_lo"]}


def to_sibling(c):
    return {**c, "core": 1 - c["core"]}


def to_home(a, e):
    return lambda c: {
        **c,
        "x_hi": c["x_hi"] ^ a,
        "core": c["x_lo"] ^ e,
        "x_lo": c["core"],
    }


FACTOR = 2.0 / HALF_WIDTH
DIAG = FACTOR * (0.5 * 7.5 - CENTER)
NEAR = FACTOR * (-0.5 * 4.0 / 3.0)
UNIT = NEAR / 16.0


def stencil_matrix():
    m = np.zeros((N, N), np.float32)
    for i in range(N):
        for d, c in ((1, 16.0), (-1, 16.0), (2, -1.0), (-2, -1.0)):
            m[i, (i + d) % N] += c
    return jnp.asarray(np.concatenate([m, m], axis=0), jnp.bfloat16)


def place_blocks(ref, target, first, z, sems, copies):
    for shift in range(4):
        where = first + 4 * lax.rem(z + 4 - shift, 4)
        copies.append(
            pltpu.make_async_copy(
                ref.at[pl.ds(4 * shift, 4)],
                target.at[pl.ds(where, 4), pl.ds(PAD, N), :],
                sems.at[len(copies)],
            )
        )


def wrap_rows(ref, p):
    ref[p, 0:PAD, :] = ref[p, N : N + PAD, :]
    ref[p, N + PAD : ROWS, :] = ref[p, PAD : 2 * PAD, :]


def products(src, along, matrix, p):
    for k in range(4):
        v = src[p + k, PAD : PAD + N, :]
        high = v.astype(jnp.bfloat16)
        low = (v - high.astype(jnp.float32)).astype(jnp.bfloat16)
        along[k] = jnp.dot(
            jnp.concatenate([high, low], axis=1),
            matrix[...],
            preferred_element_type=jnp.float32,
        )


def four_planes(src, dst, pot, along, p, first_step, out=None, places=None):
    for t in range(N // 8):
        r = PAD + 8 * t
        column = [src[p + k - 2, r : r + 8, :] for k in range(8)]
        for k in range(4):
            near = column[k + 1] + column[k + 3]
            far = column[k] + column[k + 4]
            near = near + (src[p + k, r - 1 : r + 7, :] + src[p + k, r + 1 : r + 9, :])
            far = far + (src[p + k, r - 2 : r + 6, :] + src[p + k, r + 2 : r + 10, :])
            sums = (16.0 * near - far) + along[k, 8 * t : 8 * t + 8, :]
            res = pot[p + k, r : r + 8, :] * column[k + 2] + UNIT * sums
            if first_step:
                res = 0.5 * res
            else:
                res = res - dst[p + k, r : r + 8, :]
            if out is not None:
                out[places[k], 8 * t : 8 * t + 8, :] = res
                continue
            dst[p + k, r : r + 8, :] = res
            if t == 0:
                dst[p + k, N + PAD : ROWS, :] = res
            if t == N // 8 - 1:
                dst[p + k, 0:PAD, :] = res


def advance(src, dst, pot, along, matrix, first, count, first_step, out=None):
    products(src, along[0], matrix, first)
    for group in range(count // 4):
        p = first + 4 * group
        if 4 * group + 4 < count:
            products(src, along[(group + 1) % 2], matrix, p + 4)
        places = [4 * k + group for k in range(4)]
        four_planes(src, dst, pot, along[group % 2], p, first_step, out, places)


def inner_kernel(
    place, own, sibling, own_pot, sibling_pot, matrix, edges, one, two, pot, even, odd, sems
):
    core, z = place[0], place[1]
    copies = []
    place_blocks(own, one, OWN * core, z, sems, copies)
    place_blocks(own_pot, pot, OWN * core, z, sems, copies)
    place_blocks(sibling, one, OWN * (1 - core), z, sems, copies)
    place_blocks(sibling_pot, pot, OWN * (1 - core), z, sems, copies)
    for copy in copies:
        copy.start()
    for copy in copies:
        copy.wait()

    @pl.loop(0, 2 * OWN)
    def _(p):
        wrap_rows(one, p)

    for step in range(DEGREE):
        src, dst = (one, two) if step % 2 == 1 else (two, one)
        if step > 0:
            advance(
                src, dst, pot, (even, odd), matrix, 2 * step, 2 * OWN - 4 * step, step == 1
            )

        base = 2 * step + core * (28 - 4 * step)

        @pl.loop(0, 4)
        def _(k):
            edges[4 * step + k] = dst[base + k]


def outer_kernel(
    place, outer, outer_pot, own_pot, edges, matrix, out, one, two, pot, even, odd, sems
):
    core, z = place[0], place[1]
    copies = []
    place_blocks(outer, one, 18 * core, z, sems, copies)
    place_blocks(outer_pot, pot, 18 * core, z, sems, copies)
    place_blocks(own_pot, pot, 16 - 14 * core, z, sems, copies)
    for copy in copies:
        copy.start()
    for copy in copies:
        copy.wait()

    @pl.loop(0, OWN)
    def _(p):
        wrap_rows(one, p + 18 * core)

    for step in range(1, DEGREE + 1):
        src, dst = (one, two) if step % 2 == 1 else (two, one)
        before = step - 1
        base = 16 + 2 * before - core * (2 + 4 * before)

        @pl.loop(0, 4)
        def _(k):
            src[base + k] = edges[4 * before + k]

        first = 2 * step + core * (18 - 4 * step)
        advance(
            src, dst, pot, (even, odd), matrix, first, OWN, step == 1,
            out if step == DEGREE else None,
        )


def filter_call(kernel, name, planes, places, shape, place_out, args):
    return pl.pallas_call(
        kernel,
        out_shape=jax.ShapeDtypeStruct(shape, jnp.float32),
        in_specs=[pl.BlockSpec(memory_space=pltpu.SMEM)]
        + [pl.BlockSpec(memory_space=m) for m in places]
        + [pl.BlockSpec(memory_space=pltpu.VMEM)],
        out_specs=pl.BlockSpec(memory_space=place_out),
        scratch_shapes=[pltpu.VMEM((planes, ROWS, N), jnp.float32)] * 3
        + [pltpu.VMEM((4, N, N), jnp.float32)] * 2
        + [pltpu.SemaphoreType.DMA((16,))],
        compiler_params=pltpu.CompilerParams(vmem_limit_bytes=20 << 20),
        cost_estimate=pl.CostEstimate(flops=1000, bytes_accessed=0, transcendentals=0),
        name=name,
    )(*args, stencil_matrix())


def filtered(place, own, sibling, outer, own_pot, sibling_pot, outer_pot):
    edges = filter_call(
        inner_kernel, "inner", 2 * OWN, [pl.ANY] * 4, (4 * DEGREE, ROWS, N), pltpu.VMEM,
        (place, own, sibling, own_pot, sibling_pot),
    )
    return filter_call(
        outer_kernel, "outer", 2 * OWN + 2, [pl.ANY] * 3 + [pltpu.VMEM], (OWN, N, N), pltpu.VMEM,
        (place, outer, outer_pot, own_pot, edges),
    )


def rotate_kernel(place, rotation, x, *outs):
    for n, out in enumerate(outs):
        b = place[0] ^ n

        @pl.loop(0, 4)
        def _(j, out=out, b=b):
            coeffs = [rotation[i, 4 * b + j] for i in range(16)]
            for first in range(0, N, 64):
                rows = [slice(first + 8 * u, first + 8 * u + 8) for u in range(8)]
                totals = [coeffs[0] * x[0, r, :] for r in rows]
                for i in range(1, 16):
                    totals = [a + coeffs[i] * x[i, r, :] for a, r in zip(totals, rows)]
                for a, r in zip(totals, rows):
                    out[j, r, :] = a


def rotated_parts(place, rotation, planes):
    vmem = pl.BlockSpec(memory_space=pltpu.VMEM)
    smem = pl.BlockSpec(memory_space=pltpu.SMEM)
    return pl.pallas_call(
        rotate_kernel,
        out_shape=[jax.ShapeDtypeStruct((4, N, N), jnp.float32)] * 4,
        in_specs=[smem, smem, vmem],
        out_specs=[vmem] * 4,
        compiler_params=pltpu.CompilerParams(vmem_limit_bytes=16 << 20),
        name="rotate",
    )(place, rotation, planes)


def gram_kernel(place, o0, o1, o2, o3, out, sums):
    parts = (o0, o1, o2, o3)
    sums[...] = jnp.zeros_like(sums)
    for rel in range(4):
        for j in range(4):
            row = 16 * (4 * (place[0] ^ rel) + j)
            for other in range(rel + 1):
                totals = [jnp.zeros((8, N), jnp.float32) for _ in range(4)]
                for t in range(N // 8):
                    a = parts[rel][j, 8 * t : 8 * t + 8, :]
                    totals = [
                        s + a * parts[other][k, 8 * t : 8 * t + 8, :]
                        for k, s in enumerate(totals)
                    ]
                for k in range(4):
                    total = jnp.sum(totals[k], axis=0, keepdims=True)
                    column = 4 * (place[0] ^ other) + k
                    sums[pl.ds(row + column, 1), :] = total
                    if other < rel:
                        back = 16 * column + 4 * (place[0] ^ rel) + j
                        sums[pl.ds(back, 1), :] = total
    out[:, 0, :] = lax.dot_general(
        jnp.ones((N, N), jnp.float32),
        sums[...],
        (((1,), (1,)), ((), ())),
        precision=lax.Precision.HIGHEST,
        preferred_element_type=jnp.float32,
    )


def gram_rows(place, parts):
    vmem = pl.BlockSpec(memory_space=pltpu.VMEM)
    smem = pl.BlockSpec(memory_space=pltpu.SMEM)
    return pl.pallas_call(
        gram_kernel,
        out_shape=jax.ShapeDtypeStruct((N, 1, 256), jnp.float32),
        in_specs=[smem] + [vmem] * 4,
        out_specs=vmem,
        scratch_shapes=[pltpu.VMEM((256, N), jnp.float32)],
        compiler_params=pltpu.CompilerParams(vmem_limit_bytes=16 << 20),
        name="gram",
    )(place, *parts)


def local(orbitals, potential, rotation):
    x_hi = lax.axis_index("x_hi")
    core = lax.axis_index("core")
    x_lo = lax.axis_index("x_lo")
    z = lax.axis_index("z")
    place = jnp.stack([core, z]).astype(jnp.int32)
    blocks = [
        lax.dynamic_index_in_dim(orbitals, (z + s) % 4, 0, keepdims=False) for s in range(4)
    ]
    diagonal = FACTOR * potential + DIAG
    blocks[2], diagonal = lax.optimization_barrier((blocks[2], diagonal))
    orbs = [moved(block, to_orbital(s)) for s, block in enumerate(blocks)]
    pots = [moved(diagonal, pot_to_orbital(s)) for s in range(4)]
    own = jnp.concatenate(orbs, axis=0)
    own_pot = jnp.concatenate(pots, axis=0)
    outer = moved(own, to_outer)
    late, *_ = lax.optimization_barrier((own, pots[0], pots[1]))
    sibling = moved(late, to_sibling)
    outer_pot = moved(own_pot, to_outer)
    sibling_pot = moved(own_pot, to_sibling)
    sibling, outer = lax.optimization_barrier((sibling, outer))
    mine = filtered(place, own, sibling, outer, own_pot, sibling_pot, outer_pot)
    planes = lax.all_to_all(mine, ("x_hi", "x_lo", "z"), 0, 0, tiled=True)
    base = jnp.stack([2 * x_hi + x_lo]).astype(jnp.int32)
    parts = rotated_parts(base, rotation, planes)
    home = [moved(parts[2 * a + e], to_home(a, e)) for a in range(2) for e in range(2)]
    parts, home[0] = lax.optimization_barrier((parts, home[0]))
    rows = lax.all_to_all(gram_rows(base, parts), AXES, 0, 0, tiled=True)
    total = jnp.sum(rows, axis=(0, 1))
    total = total.reshape(16, 16) / (N * N * N)
    correlation = lax.dynamic_slice_in_dim(total, 4 * (2 * x_hi + core), 4, 0)
    band = 2 * x_hi + core
    pieces = []
    for p in range(4):
        rel = band ^ p
        piece = jnp.where(
            rel < 2,
            jnp.where(rel == 0, home[0], home[1]),
            jnp.where(rel == 2, home[2], home[3]),
        )
        pieces.append(piece)
    return jnp.stack(pieces, axis=1), correlation


def solution(mesh):
    fine = Mesh(mesh.devices.reshape(SIZES), AXES)
    band, dom = ("x_hi", "core"), ("y", "x_lo", "z")
    return jax.shard_map(
        local,
        mesh=fine,
        in_specs=(P(band, dom, None, None), P(dom, None, None), P()),
        out_specs=(P(band, dom, None, None), P(band, None)),
        check_vma=False,
    )
```

```python
import jax
import jax.numpy as jnp
import numpy as np
from jax import lax
from jax.experimental import pallas as pl
from jax.experimental.pallas import tpu as pltpu
from jax.sharding import Mesh, PartitionSpec as P

DEGREE = 8
CENTER = 4.5
HALF_WIDTH = 5.0
AXES = ("x_hi", "core", "y", "x_lo", "z")
SIZES = (2, 2, 4, 2, 4)
N = 128
PAD = 8
ROWS = N + 2 * PAD
OWN = 16


def moved(array, where):
    pairs = []
    for i in range(int(np.prod(SIZES))):
        c = dict(zip(AXES, (int(k) for k in np.unravel_index(i, SIZES))))
        d = where(c)
        j = int(np.ravel_multi_index([d[a] % s for a, s in zip(AXES, SIZES)], SIZES))
        pairs.append((i, j))
    return lax.ppermute(array, AXES, pairs)


def to_orbital(shift):
    return lambda c: {**c, "core": c["x_lo"], "x_lo": c["core"], "z": c["z"] + shift}


def to_outer(c):
    return {**c, "core": 1 - c["core"], "y": c["y"] + (1 if c["core"] == 1 else -1)}


def pot_to_orbital(shift):
    return lambda c: {**to_orbital(shift)(c), "x_hi": c["x_hi"] ^ c["core"] ^ c["x_lo"]}


def to_sibling(c):
    return {**c, "core": 1 - c["core"]}


def to_home(a, e):
    return lambda c: {
        **c,
        "x_hi": c["x_hi"] ^ a,
        "core": c["x_lo"] ^ e,
        "x_lo": c["core"],
    }


FACTOR = 2.0 / HALF_WIDTH
DIAG = FACTOR * (0.5 * 7.5 - CENTER)
NEAR = FACTOR * (-0.5 * 4.0 / 3.0)
UNIT = NEAR / 16.0


def stencil_matrix():
    m = np.zeros((N, N), np.float32)
    for i in range(N):
        for d, c in ((1, 16.0), (-1, 16.0), (2, -1.0), (-2, -1.0)):
            m[i, (i + d) % N] += c
    return jnp.asarray(np.concatenate([m, m], axis=0), jnp.bfloat16)


def place_blocks(ref, target, first, z, sems, copies):
    for shift in range(4):
        where = first + 4 * lax.rem(z + 4 - shift, 4)
        copies.append(
            pltpu.make_async_copy(
                ref.at[pl.ds(4 * shift, 4)],
                target.at[pl.ds(where, 4), pl.ds(PAD, N), :],
                sems.at[len(copies)],
            )
        )


def wrap_rows(ref, p):
    ref[p, 0:PAD, :] = ref[p, N : N + PAD, :]
    ref[p, N + PAD : ROWS, :] = ref[p, PAD : 2 * PAD, :]


def products(src, along, matrix, p):
    for k in range(4):
        v = src[p + k, PAD : PAD + N, :]
        high = v.astype(jnp.bfloat16)
        low = (v - high.astype(jnp.float32)).astype(jnp.bfloat16)
        along[k] = jnp.dot(
            jnp.concatenate([high, low], axis=1),
            matrix[...],
            preferred_element_type=jnp.float32,
        )


def four_planes(src, dst, pot, along, p, first_step, out=None, places=None):
    for t in range(N // 8):
        r = PAD + 8 * t
        column = [src[p + k - 2, r : r + 8, :] for k in range(8)]
        for k in range(4):
            near = column[k + 1] + column[k + 3]
            far = column[k] + column[k + 4]
            near = near + (src[p + k, r - 1 : r + 7, :] + src[p + k, r + 1 : r + 9, :])
            far = far + (src[p + k, r - 2 : r + 6, :] + src[p + k, r + 2 : r + 10, :])
            sums = (16.0 * near - far) + along[k, 8 * t : 8 * t + 8, :]
            res = pot[p + k, r : r + 8, :] * column[k + 2] + UNIT * sums
            if first_step:
                res = 0.5 * res
            else:
                res = res - dst[p + k, r : r + 8, :]
            if out is not None:
                out[places[k], 8 * t : 8 * t + 8, :] = res
                continue
            dst[p + k, r : r + 8, :] = res
            if t == 0:
                dst[p + k, N + PAD : ROWS, :] = res
            if t == N // 8 - 1:
                dst[p + k, 0:PAD, :] = res


def advance(src, dst, pot, along, matrix, first, count, first_step, out=None):
    products(src, along[0], matrix, first)
    for group in range(count // 4):
        p = first + 4 * group
        if 4 * group + 4 < count:
            products(src, along[(group + 1) % 2], matrix, p + 4)
        places = [4 * k + group for k in range(4)]
        four_planes(src, dst, pot, along[group % 2], p, first_step, out, places)


def inner_kernel(
    place, own, sibling, own_pot, sibling_pot, matrix, edges, one, two, pot, even, odd, sems
):
    core, z = place[0], place[1]
    copies = []
    place_blocks(own, one, OWN * core, z, sems, copies)
    place_blocks(own_pot, pot, OWN * core, z, sems, copies)
    place_blocks(sibling, one, OWN * (1 - core), z, sems, copies)
    place_blocks(sibling_pot, pot, OWN * (1 - core), z, sems, copies)
    for copy in copies:
        copy.start()
    for copy in copies:
        copy.wait()

    @pl.loop(0, 2 * OWN)
    def _(p):
        wrap_rows(one, p)

    for step in range(DEGREE):
        src, dst = (one, two) if step % 2 == 1 else (two, one)
        if step > 0:
            advance(
                src, dst, pot, (even, odd), matrix, 2 * step, 2 * OWN - 4 * step, step == 1
            )

        base = 2 * step + core * (28 - 4 * step)

        @pl.loop(0, 4)
        def _(k):
            edges[4 * step + k] = dst[base + k]


def outer_kernel(
    place, outer, outer_pot, own_pot, edges, matrix, out, one, two, pot, even, odd, sems
):
    core, z = place[0], place[1]
    copies = []
    place_blocks(outer, one, 18 * core, z, sems, copies)
    place_blocks(outer_pot, pot, 18 * core, z, sems, copies)
    place_blocks(own_pot, pot, 16 - 14 * core, z, sems, copies)
    for copy in copies:
        copy.start()
    for copy in copies:
        copy.wait()

    @pl.loop(0, OWN)
    def _(p):
        wrap_rows(one, p + 18 * core)

    for step in range(1, DEGREE + 1):
        src, dst = (one, two) if step % 2 == 1 else (two, one)
        before = step - 1
        base = 16 + 2 * before - core * (2 + 4 * before)

        @pl.loop(0, 4)
        def _(k):
            src[base + k] = edges[4 * before + k]

        first = 2 * step + core * (18 - 4 * step)
        advance(
            src, dst, pot, (even, odd), matrix, first, OWN, step == 1,
            out if step == DEGREE else None,
        )


def filter_call(kernel, name, planes, places, shape, place_out, args):
    return pl.pallas_call(
        kernel,
        out_shape=jax.ShapeDtypeStruct(shape, jnp.float32),
        in_specs=[pl.BlockSpec(memory_space=pltpu.SMEM)]
        + [pl.BlockSpec(memory_space=m) for m in places]
        + [pl.BlockSpec(memory_space=pltpu.VMEM)],
        out_specs=pl.BlockSpec(memory_space=place_out),
        scratch_shapes=[pltpu.VMEM((planes, ROWS, N), jnp.float32)] * 3
        + [pltpu.VMEM((4, N, N), jnp.float32)] * 2
        + [pltpu.SemaphoreType.DMA((16,))],
        compiler_params=pltpu.CompilerParams(vmem_limit_bytes=20 << 20),
        cost_estimate=pl.CostEstimate(flops=1000, bytes_accessed=0, transcendentals=0),
        name=name,
    )(*args, stencil_matrix())


def filtered(place, own, sibling, outer, own_pot, sibling_pot, outer_pot):
    edges = filter_call(
        inner_kernel, "inner", 2 * OWN, [pl.ANY] * 4, (4 * DEGREE, ROWS, N), pltpu.VMEM,
        (place, own, sibling, own_pot, sibling_pot),
    )
    return filter_call(
        outer_kernel, "outer", 2 * OWN + 2, [pl.ANY] * 3 + [pltpu.VMEM], (OWN, N, N), pltpu.VMEM,
        (place, outer, outer_pot, own_pot, edges),
    )


def rotate_kernel(place, rotation, x, *outs):
    for n, out in enumerate(outs):
        b = place[0] ^ n

        @pl.loop(0, 4)
        def _(j, out=out, b=b):
            coeffs = [rotation[i, 4 * b + j] for i in range(16)]
            for first in range(0, N, 64):
                rows = [slice(first + 8 * u, first + 8 * u + 8) for u in range(8)]
                totals = [coeffs[0] * x[0, r, :] for r in rows]
                for i in range(1, 16):
                    totals = [a + coeffs[i] * x[i, r, :] for a, r in zip(totals, rows)]
                for a, r in zip(totals, rows):
                    out[j, r, :] = a


def rotated_parts(place, rotation, planes):
    vmem = pl.BlockSpec(memory_space=pltpu.VMEM)
    smem = pl.BlockSpec(memory_space=pltpu.SMEM)
    return pl.pallas_call(
        rotate_kernel,
        out_shape=[jax.ShapeDtypeStruct((4, N, N), jnp.float32)] * 4,
        in_specs=[smem, smem, vmem],
        out_specs=[vmem] * 4,
        compiler_params=pltpu.CompilerParams(vmem_limit_bytes=16 << 20),
        name="rotate",
    )(place, rotation, planes)


def gram_kernel(place, o0, o1, o2, o3, out, sums):
    parts = (o0, o1, o2, o3)
    sums[...] = jnp.zeros_like(sums)
    for rel in range(4):
        for j in range(4):
            row = 16 * (4 * (place[0] ^ rel) + j)
            for other in range(rel + 1):
                totals = [jnp.zeros((8, N), jnp.float32) for _ in range(4)]
                for t in range(N // 8):
                    a = parts[rel][j, 8 * t : 8 * t + 8, :]
                    totals = [
                        s + a * parts[other][k, 8 * t : 8 * t + 8, :]
                        for k, s in enumerate(totals)
                    ]
                for k in range(4):
                    total = jnp.sum(totals[k], axis=0, keepdims=True)
                    column = 4 * (place[0] ^ other) + k
                    sums[pl.ds(row + column, 1), :] = total
                    if other < rel:
                        back = 16 * column + 4 * (place[0] ^ rel) + j
                        sums[pl.ds(back, 1), :] = total
    out[:, 0, :] = lax.dot_general(
        jnp.ones((N, N), jnp.float32),
        sums[...],
        (((1,), (1,)), ((), ())),
        precision=lax.Precision.HIGHEST,
        preferred_element_type=jnp.float32,
    )


def gram_rows(place, parts):
    vmem = pl.BlockSpec(memory_space=pltpu.VMEM)
    smem = pl.BlockSpec(memory_space=pltpu.SMEM)
    return pl.pallas_call(
        gram_kernel,
        out_shape=jax.ShapeDtypeStruct((N, 1, 256), jnp.float32),
        in_specs=[smem] + [vmem] * 4,
        out_specs=vmem,
        scratch_shapes=[pltpu.VMEM((256, N), jnp.float32)],
        compiler_params=pltpu.CompilerParams(vmem_limit_bytes=16 << 20),
        name="gram",
    )(place, *parts)


def local(orbitals, potential, rotation):
    x_hi = lax.axis_index("x_hi")
    core = lax.axis_index("core")
    x_lo = lax.axis_index("x_lo")
    z = lax.axis_index("z")
    place = jnp.stack([core, z]).astype(jnp.int32)
    blocks = [
        lax.dynamic_index_in_dim(orbitals, (z + s) % 4, 0, keepdims=False) for s in range(4)
    ]
    diagonal = FACTOR * potential + DIAG
    blocks[2], diagonal = lax.optimization_barrier((blocks[2], diagonal))
    orbs = [moved(block, to_orbital(s)) for s, block in enumerate(blocks)]
    orbs[0], diagonal = lax.optimization_barrier((orbs[0], diagonal))
    pots = [moved(diagonal, pot_to_orbital(s)) for s in range(4)]
    own = jnp.concatenate(orbs, axis=0)
    own_pot = jnp.concatenate(pots, axis=0)
    outer = moved(own, to_outer)
    late, *_ = lax.optimization_barrier((own, pots[0], pots[1]))
    sibling = moved(late, to_sibling)
    outer_pot = moved(own_pot, to_outer)
    sibling_pot = moved(own_pot, to_sibling)
    sibling, outer = lax.optimization_barrier((sibling, outer))
    mine = filtered(place, own, sibling, outer, own_pot, sibling_pot, outer_pot)
    planes = lax.all_to_all(mine, ("x_hi", "x_lo", "z"), 0, 0, tiled=True)
    base = jnp.stack([2 * x_hi + x_lo]).astype(jnp.int32)
    parts = rotated_parts(base, rotation, planes)
    home = [moved(parts[2 * a + e], to_home(a, e)) for a in range(2) for e in range(2)]
    parts, home[0] = lax.optimization_barrier((parts, home[0]))
    rows = lax.all_to_all(gram_rows(base, parts), AXES, 0, 0, tiled=True)
    total = jnp.sum(rows, axis=(0, 1))
    total = total.reshape(16, 16) / (N * N * N)
    correlation = lax.dynamic_slice_in_dim(total, 4 * (2 * x_hi + core), 4, 0)
    band = 2 * x_hi + core
    pieces = []
    for p in range(4):
        rel = band ^ p
        piece = jnp.where(
            rel < 2,
            jnp.where(rel == 0, home[0], home[1]),
            jnp.where(rel == 2, home[2], home[3]),
        )
        pieces.append(piece)
    return jnp.stack(pieces, axis=1), correlation


def solution(mesh):
    fine = Mesh(mesh.devices.reshape(SIZES), AXES)
    band, dom = ("x_hi", "core"), ("y", "x_lo", "z")
    return jax.shard_map(
        local,
        mesh=fine,
        in_specs=(P(band, dom, None, None), P(dom, None, None), P()),
        out_specs=(P(band, dom, None, None), P(band, None)),
        check_vma=False,
    )
```
